32 devices in a mesh: gx: 4 (over x, core), gy: 4 (over z), gz: 2 (over y).
Axes of the slice: x: 2, y: 2, z: 4, core: 2. Of those that a mesh axis runs over, the one named last changes fastest.
Arguments:
- displacement: float32 [3, 32, 32, 256], P(None, 'gx', 'gy', 'gz'), may hold values from -0.25 to 0.25
- bond_intact: int32 [61, 32, 32, 256], P(None, 'gx', 'gy', 'gz'), may hold values 0 or 1
Outputs:
- force: float32 [3, 32, 32, 256], P(None, 'gx', 'gy', 'gz')
- dilatation: float32 [32, 32, 256], P('gx', 'gy', 'gz')
The draws below stay inside these ranges and needn't reach their ends.
All inputs are finite; a program needn't handle non-finite values. No bound on the sum of `bond_intact` on one device may be relied on, other than what follows from the above.
Results may differ from the reference program's by a relative error of at most 0.000063.
Values sent between devices are 32-bit elements; how exact they have to be, the bound alone decides.
A program may use at most 128 MiB of HBM per device.

```python
import math
import jax
import jax.numpy as jnp
from jax import lax

HALF_BONDS = 61
NX = 32
NY = 32
NZ = 256


def set_ends(result, own_key, least, high):
    index_at = [jax.random.randint(jax.random.fold_in(own_key, axis), (), 0, length) for axis, length in enumerate(result.shape)]
    widest = result.shape.index(max(result.shape))
    beside = index_at[:widest] + [(index_at[widest] + 1) % result.shape[widest]] + index_at[widest + 1:]
    return result.at[tuple(index_at)].set(least).at[tuple(beside)].set(high)


def shard_levels(key, shape, split, low, high):
    factor_of, own = 1.0, jax.random.fold_in(key, 6)
    for position, parts in split:
        heights = jnp.exp(jax.random.uniform(jax.random.fold_in(own, position), (parts,), jnp.float32, low / len(split), high / len(split)))
        factor_of = factor_of * jnp.repeat(heights, shape[position] // parts).reshape([-1 if axis == position else 1 for axis in range(len(shape))])
    return factor_of


def bell_draw(key, dims, scale, most, cuts=(), dtype=jnp.bfloat16):
    entries = scale * jax.random.normal(key, dims, jnp.float32)
    if cuts:
        entries = entries * shard_levels(key, dims, cuts, -0.22, 0.18)
    return jnp.clip(entries, -most, most).astype(dtype)


def setup_inputs(seed: int = 0) -> dict:
    key_list = jax.random.split(jax.random.key(seed), 3)
    displacement = bell_draw(key_list[0], (3, NX, NY, NZ), 0.05, 0.25, ((1, 4), (2, 4), (3, 2)), jnp.float32)
    bond_intact = set_ends((jax.random.randint(key_list[1], (HALF_BONDS, NX, NY, NZ), 0, 8) < 7).astype(jnp.int32), jax.random.fold_in(key_list[1], 1), 0, 1)
    return dict(displacement=displacement, bond_intact=bond_intact)


bulk_modulus = 150.0
shear_modulus = 25.0
soft_stretch = 0.05

def bond_offsets():
    chosen = []
    for step_x in range(0, 4):
        for step_y in range(-3, 4):
            for step_z in range(-3, 4):
                if step_x * step_x + step_y * step_y + step_z * step_z > 9:
                    continue
                if step_x > 0 or (step_x == 0 and (step_y > 0 or (step_y == 0 and step_z > 0))):
                    chosen.append((step_x, step_y, step_z))
    return chosen

def weighted_volume():
    total = 0.0
    for offset in bond_offsets():
        squared = offset[0] * offset[0] + offset[1] * offset[1] + offset[2] * offset[2]
        total = total + math.exp(-squared / 9.0) * squared
    return 2.0 * total

def offset_terms(offset):
    squared = offset[0] * offset[0] + offset[1] * offset[1] + offset[2] * offset[2]
    return (math.sqrt(squared), math.exp(-squared / 9.0))

def bond_vector(owner_u, partner_u, offset):
    pieces = [offset[number] + partner_u[number] - owner_u[number] for number in range(3)]
    length = jnp.sqrt(pieces[0] * pieces[0] + pieces[1] * pieces[1] + pieces[2] * pieces[2])
    return (pieces, length)

def dilatation_term(length, offset, intact, volume):
    radius, weight = offset_terms(offset)
    return intact * (3.0 / volume * weight * radius) * (length - radius)

def force_scalar(length, offset, theta_owner, theta_partner, intact, volume):
    radius, weight = offset_terms(offset)
    both = theta_owner + theta_partner
    extension = length - radius
    ratio = extension / (radius * soft_stretch)
    soften = 1.0 / (1.0 + ratio * ratio)
    total = 3.0 * bulk_modulus / volume * weight * radius * both + 15.0 * shear_modulus / volume * weight * (2.0 * extension - both * (radius / 3.0))
    return intact * soften * total / length

def window(array, offset, extent):
    return array[..., 3 + offset[0]:3 + offset[0] + extent[0], 3 + offset[1]:3 + offset[1] + extent[1], 3 + offset[2]:3 + offset[2] + extent[2]]

def add_block(target, block, offset):
    starts = (0,) * (target.ndim - 3) + tuple((3 + shift_step for shift_step in offset))
    current = lax.dynamic_slice(target, starts, block.shape)
    return lax.dynamic_update_slice(target, current + block, starts)

def reference(displacement, bond_intact):
    offsets = bond_offsets()
    volume = weighted_volume()
    extent = displacement.shape[1:]
    pad_u = jnp.pad(displacement, ((0, 0), (3, 3), (3, 3), (3, 3)))
    exists = jnp.pad(jnp.ones(extent, jnp.float32), 3)
    anchor = (0, 0, 0)
    theta_sum = jnp.zeros(exists.shape, jnp.float32)
    for bond_index, offset in enumerate(offsets):
        intact = bond_intact[bond_index].astype(jnp.float32) * window(exists, offset, extent)
        pieces, length = bond_vector(displacement, window(pad_u, offset, extent), offset)
        term = dilatation_term(length, offset, intact, volume)
        theta_sum = add_block(theta_sum, term, anchor)
        theta_sum = add_block(theta_sum, term, offset)
    theta = theta_sum[3:-3, 3:-3, 3:-3]
    pad_theta = jnp.pad(theta, 3)
    force_sum = jnp.zeros((3,) + exists.shape, jnp.float32)
    for bond_index, offset in enumerate(offsets):
        intact = bond_intact[bond_index].astype(jnp.float32) * window(exists, offset, extent)
        pieces, length = bond_vector(displacement, window(pad_u, offset, extent), offset)
        scalar = force_scalar(length, offset, theta, window(pad_theta, offset, extent), intact, volume)
        push = jnp.stack([scalar * piece for piece in pieces])
        force_sum = add_block(force_sum, push, anchor)
        force_sum = add_block(force_sum, -push, offset)
    return (force_sum[:, 3:-3, 3:-3, 3:-3], theta)
```

```python
import functools
import math

import jax
import jax.numpy as jnp
from jax import lax
from jax.experimental import pallas as pl
from jax.experimental.pallas import tpu as pltpu
from jax.sharding import PartitionSpec as P

MESH = pl.DeviceIdType.MESH
bulk_modulus = 150.0
shear_modulus = 25.0
soft_stretch = 0.05
AXES = ("gx", "gy", "gz")
H = 3
PAD = 4
GROUP = 8


def bond_offsets():
    chosen = []
    for step_x in range(0, 4):
        for step_y in range(-3, 4):
            for step_z in range(-3, 4):
                if step_x * step_x + step_y * step_y + step_z * step_z > 9:
                    continue
                if step_x > 0 or (step_x == 0 and (step_y > 0 or (step_y == 0 and step_z > 0))):
                    chosen.append((step_x, step_y, step_z))
    return chosen


OFFSETS = bond_offsets()
NUMBER = {o: k for k, o in enumerate(OFFSETS)}
ORDER = sorted(range(len(OFFSETS)), key=lambda k: (OFFSETS[k][:2], OFFSETS[k][2]))


def square(offset):
    return sum(step * step for step in offset)


VOLUME = 2.0 * sum(math.exp(-square(o) / 9.0) * square(o) for o in OFFSETS)


def minus(offset):
    return tuple(-step for step in offset)


def bond_of(step):
    return (NUMBER[step], True) if step in NUMBER else (NUMBER[minus(step)], False)


def radius_of(k):
    return math.sqrt(square(OFFSETS[k]))


def terms(k):
    weight, radius = math.exp(-square(OFFSETS[k]) / 9.0), radius_of(k)
    c = 3.0 / VOLUME * weight * radius
    a = 3.0 * bulk_modulus / VOLUME * weight * radius
    b = 15.0 * shear_modulus / VOLUME * weight
    return c, (a - b * radius / 3.0) / c, 2.0 * b / c


STEPS = [s for o in OFFSETS for s in (o, minus(o))]
PAIRS = sorted({s[1:] for s in STEPS})
FIRST = {}
LAST = {}
for _k, _o in enumerate(OFFSETS):
    FIRST.setdefault(_o[0], _k)
    LAST[_o[0]] = _k + 1
RUNS = {}
for _k, _o in enumerate(OFFSETS):
    if _o[1]:
        RUNS.setdefault(_o[:2], []).append(_k)
RUNS = {g: (ks[0], ks[-1] + 1) for g, ks in RUNS.items()}

SLOTS = sorted(
    {(o[0], o[1], abs(o[2])) for o in OFFSETS if o[2]},
    key=lambda s: ((0 if s[1] > 0 else 1 if s[1] < 0 else 2), s[0] if s[1] else -s[0], s),
)
SLOT = {s: i for i, s in enumerate(SLOTS)}
STRIP = sorted({(s[0], s[1], abs(s[2])) for s in STEPS if s[2]})
MOVES = sorted({(s[0], s[2]) for s in STRIP})


def span(test):
    found = [i for i, s in enumerate(SLOTS) if test(s)]
    assert found == list(range(found[0], found[-1] + 1))
    return slice(found[0], found[-1] + 1)


def side(step, size, at):
    return slice(at - H, at) if step < 0 else slice(at + size, at + size + H) if step > 0 else slice(at, at + size)


def edge_of(step, size, at):
    return slice(at, at + H) if step < 0 else slice(at + size - H, at + size) if step > 0 else slice(at, at + size)


def evaluations(bx, by):
    x_list, y_list = [], []
    for x in range(bx):
        x_list += [("x", x, s) for s in sorted(STEPS, key=lambda s: (s[1], s[2])) if not 0 <= x + s[0] < bx]
    for r in range(by):
        y_list += [("y", r, s) for s in sorted(STEPS, key=lambda s: (s[0], s[2])) if not 0 <= r + s[1] < by]
    return x_list, y_list, [("z", 0, s) for s in STRIP]


def scratch_plan(bonds, bx, by, bz):
    rows, planes, f, i = by + 2 * PAD, 2 * bx, jnp.float32, jnp.int32
    halo = sum(len(part) for part in evaluations(bx, by))
    plan = {"jf": (f, (bonds, bx, by, bz)), "ext": (f, (bonds, bx, by, bz)), "len": (f, (bonds, bx, by, bz))}
    plan["d"] = (f, (bonds, bx, 3, by, bz))
    plan["hj"] = plan["hext"] = plan["hlen"] = (f, (halo, by, bz))
    plan["hd"] = (f, (halo, 3, by, bz))
    plan["mask"] = (f, (len(PAIRS), by, bz))
    plan["lanes"] = (f, (7, by, bz))
    plan["ix"] = (i, (bonds, H, rows, bz))
    plan["iy"] = (i, (bonds, bx, by, bz))
    plan["own_slots"] = (f, (len(SLOTS), by, bz))
    plan["slots"] = (f, (2, 2, len(SLOTS), rows, bz))
    for name, c in (("u", 3), ("t", 1)):
        plan[name, "field"] = (f, (c, planes, rows, bz))
        plan[name, "main"] = (f, (7, c, bx + H, rows, bz))
        plan[name, "sums"] = (f, (7, bx + H, c, rows, bz))
        plan[name, "base"] = (f, (c, bx, by, bz))
        plan[name, "x"] = (f, (7, c, 2 * H, rows, bz))
        plan[name, "y"] = (f, (7, c, 2 * H, planes, bz))
        plan[name, "in"] = (f, (c, by, bz))
        plan[name, "z"] = (f, (2, 3, c, rows, bz))
        plan[name, "q"] = (f, (len(MOVES), c, rows, bz))
    return plan


def kernel(sizes, names, u_hbm, intact_hbm, force_out, theta_out, *scratch):
    B = dict(zip(names, scratch))
    intact, send_sem, recv_sem, load_sem = scratch[len(names) :]
    bx, by, bz = theta_out.shape
    rows, planes = by + 2 * PAD, 2 * bx
    assert bx == by and planes * GROUP == bz and GROUP >= 2 * H + 2
    x_list, y_list, z_list = evaluations(bx, by)
    everything = x_list + y_list + z_list
    place = {e: i for i, e in enumerate(everything)}
    index = {a: lax.axis_index(a) for a in AXES}
    has = {(a, -1): index[a] > 0 for a in AXES}
    has.update({(a, 1): index[a] < sizes[a] - 1 for a in AXES})
    own = slice(PAD, PAD + by)

    def there(direction):
        found = None
        for a, step in zip(AXES, direction):
            if step:
                found = has[a, step] if found is None else found & has[a, step]
        return found

    everyone = [(x, y, z) for x in (-1, 0, 1) for y in (-1, 0, 1) for z in (-1, 0, 1) if x or y or z]
    exists = {d: there(d) for d in everyone}

    def device(direction):
        return {a: index[a] + step for a, step in zip(AXES, direction) if step}

    u = B["u", "field"]
    load_u = pltpu.make_async_copy(u_hbm, u.at[:, H : H + bx, own, :], load_sem.at[0])
    load_u.start()
    load = pltpu.make_async_copy(intact_hbm, intact, load_sem.at[1])
    load.start()

    barrier = pltpu.get_barrier_semaphore()
    count = jnp.int32(0)
    for d in everyone:
        count = count + jnp.where(exists[d], 1, 0).astype(jnp.int32)

        @pl.when(exists[d])
        def _(d=d):
            pl.semaphore_signal(barrier, inc=1, device_id=device(d), device_id_type=MESH)

    copies = []

    class Shift:
        def __init__(self, direction, src, dst):
            number = len(copies)
            copies.append(self)
            self.direction = direction
            self.copy = pltpu.make_async_remote_copy(
                src_ref=src, dst_ref=dst, send_sem=send_sem.at[number], recv_sem=recv_sem.at[number],
                device_id=device(direction), device_id_type=MESH,
            )
            self.sends = exists[direction]
            self.takes = exists[minus(direction)]

            @pl.when(self.sends)
            def _():
                self.copy.start()

        def receive(self):
            @pl.when(self.takes)
            def _():
                self.copy.wait_recv()

        def finish(self):
            @pl.when(self.sends)
            def _():
                self.copy.wait_send()

    def nothing(view):
        view[...] = jnp.zeros(view.shape, view.dtype)

    def landing(name, d):
        if d[2]:
            return B[name, "z"].at[(d[2] + 1) // 2, d[0] + 1, :, side(d[1], by, PAD), :]
        return B[name, "field"].at[:, side(d[0], bx, H), side(d[1], by, PAD), :]

    SENT = (slice(0, by), slice(by - 2, by), slice(0, 2))
    LAND = (slice(PAD, PAD + by), slice(PAD - 2, PAD), slice(PAD + by, PAD + by + 2))
    up, down = span(lambda s: s[1] > 0), span(lambda s: s[1] < 0)
    x_all, x_up = span(lambda s: s[0] > 0), span(lambda s: s[0] > 0 and s[1] > 0)
    slot_moves = []
    for dz in (-1, 1):
        for dx, parts in ((0, (slice(0, len(SLOTS)), up, down)), (1, (x_all, x_up, down))):
            for way, dy in enumerate((0, 1, -1)):
                slot_moves.append(((dx, dy, dz), parts[way], way))

    def slot_landing(d, part, way):
        return B["slots"].at[(1 - d[2]) // 2, d[0], part, LAND[way], :]

    for d in everyone:

        @pl.when(jnp.logical_not(exists[d]))
        def _(d=d):
            for name in ("u", "t"):
                nothing(landing(name, d))
            for e, part, way in slot_moves:
                if minus(e) == d:
                    nothing(slot_landing(e, part, way))
            if d == (-1, 0, 0):
                nothing(B["ix"])
            for (ex, ey), (k0, k1) in RUNS.items():
                back = -1 if ey > 0 else 1
                at = slice(by - ey, by) if ey > 0 else slice(0, -ey)
                if d == (0, back, 0):
                    nothing(B["iy"].at[k0:k1, ex:, at, :])
                if ex and d == (-1, back, 0):
                    nothing(B["iy"].at[k0:k1, 0:ex, at, :])

    lane = lax.broadcasted_iota(jnp.int32, (by, bz), 1)
    row = lax.broadcasted_iota(jnp.int32, (by, bz), 0)
    spot = lax.rem(lane, GROUP)
    high = spot >= GROUP // 2
    edge = (lane < H) | (lane >= bz - H)
    inner = (lane >= H * GROUP) & (lane < (H + bx) * GROUP)
    zero = jnp.zeros((by, bz), jnp.float32)

    def number(condition):
        return jnp.where(condition, 1.0, 0.0)

    def roll(value, amount):
        return pltpu.roll(value, amount % bz, 1) if amount % bz else value

    def to_strip(total):
        return jnp.where(high, roll(total, GROUP), total)

    def pack(tiles):
        total = zero
        for x, tile in enumerate(tiles):
            total = total + roll(jnp.where(edge, tile, 0.0), GROUP * (x + H))
        return to_strip(total)

    def unpack(strip):
        strip = jnp.where(high, roll(strip, -GROUP), strip)
        return [jnp.where(edge, roll(strip, -GROUP * (x + H)), 0.0) for x in range(bx)]

    def flat(ref, *at):
        return ref.reshape(*ref.shape[:-3], ref.shape[-3] * ref.shape[-2], bz)

    u_flat, t_flat, intact_flat = flat(u), flat(B["t", "field"]), flat(intact)
    iy_flat = flat(B["iy"])

    def clear(ref, depth):
        zeros = jnp.zeros(ref.shape[2:], jnp.float32)

        def body(i, carry):
            for s in range(depth):
                ref[s, i] = zeros
            return carry

        lax.fori_loop(0, ref.shape[1], body, 0)

    for name in ("u", "t"):
        main, beside = B[name, "main"], B[name, "x"]
        for c in range(main.shape[1]):
            for s in range(7):

                def blank(i, carry, s=s, c=c, main=main):
                    main[s, c, i] = jnp.zeros((rows, bz), jnp.float32)
                    return carry

                lax.fori_loop(0, bx + H, blank, 0)

                def blank_x(i, carry, s=s, c=c, beside=beside):
                    beside[s, c, i] = jnp.zeros((rows, bz), jnp.float32)
                    return carry

                lax.fori_loop(0, 2 * H, blank_x, 0)
    clear(B["t", "sums"], 7)
    clear(B["u", "sums"], 7)

    for i, (ey, ez) in enumerate(PAIRS):
        B["mask"][i] = number((row + ey >= 0) & (row + ey < by) & (lane + ez >= 0) & (lane + ez < bz))
    for ez in range(-H, H + 1):
        B["lanes"][ez + H] = number((lane + ez >= 0) & (lane + ez < bz))

    def mask(ey, ez):
        return B["mask"][PAIRS.index((ey, ez))]

    def shift_main(name):
        field, out = B[name, "field"], B[name, "main"]
        for c in range(field.shape[0]):

            def body(x, carry, c=c):
                value = field[c, x + H, own, :]
                for ez in range(-H, H + 1):
                    out[ez + H, c, x, own, :] = roll(value, -ez)
                return carry

            lax.fori_loop(0, bx, body, 0)

    load_u.wait()
    for c in range(3):
        B["u", "in"][c] = pack([u[c, x + H, own, :] for x in range(bx)])
    load.wait()

    beyond_x = number(has["gx", 1])
    z_up, z_down = number(has["gz", 1]), number(has["gz", -1])

    def slots_body(x, totals):
        new = []
        crossing = jnp.where(has["gx", 1], 1.0, 0.0)
        for (ex, ey, az), total in zip(SLOTS, totals):
            value = jnp.where(lane >= bz - az, intact[NUMBER[ex, ey, az], x].astype(jnp.float32) * z_up, 0.0)
            if (ex, ey, -az) in NUMBER:
                other = intact[NUMBER[ex, ey, -az], x].astype(jnp.float32) * z_down
                value = jnp.where(lane < az, other, value)
            if ex:
                value = value * jnp.where(x + ex < bx, 1.0, crossing)
            new.append(total + pltpu.roll(value, GROUP * (x + H), 1))
        return tuple(new)

    totals = lax.fori_loop(0, bx, slots_body, tuple(zero for _ in SLOTS))
    y_inside = {}
    for ey in range(-H, H + 1):
        inside = (row + ey >= 0) & (row + ey < by)
        y_inside[ey] = jnp.where(inside, 1.0, number(has["gy", 1 if ey > 0 else -1])) if ey else None
    for (ex, ey, az), total in zip(SLOTS, totals):
        value = to_strip(total) * terms(NUMBER[ex, ey, az])[0]
        B["own_slots"][SLOT[ex, ey, az]] = value * y_inside[ey] if ey else value

    pl.semaphore_wait(barrier, count)

    def spread(name, far=False):
        field, strip = B[name, "field"], B[name, "in"]
        sent = []
        for d in sorted(everyone, key=lambda d: -sum(map(abs, d))):
            if d[2]:
                src = strip.at[:, edge_of(d[1], by, 0), :]
            else:
                src = field.at[:, edge_of(d[0], bx, H), edge_of(d[1], by, PAD), :]
            sent.append(Shift(d, src, landing(name, minus(d))))
        return sent

    sent_u = spread("u")
    sent_i = []
    for (ex, ey), (k0, k1) in RUNS.items():
        toward = 1 if ey > 0 else -1
        at = slice(by - ey, by) if ey > 0 else slice(0, -ey)
        if ex:
            sent_i.append(
                Shift((1, toward, 0), intact.at[k0:k1, bx - ex :, at, :], B["iy"].at[k0:k1, 0:ex, at, :])
            )
    for e, part, way in reversed(slot_moves):
        sent_i.append(Shift(e, B["own_slots"].at[part, SENT[way], :], slot_landing(e, part, way)))
    for (ex, ey), (k0, k1) in RUNS.items():
        toward = 1 if ey > 0 else -1
        at = slice(by - ey, by) if ey > 0 else slice(0, -ey)
        sent_i.append(
            Shift((0, toward, 0), intact.at[k0:k1, 0 : bx - ex, at, :], B["iy"].at[k0:k1, ex:, at, :])
        )
    for ex in range(1, H + 1):
        k0, k1 = FIRST[ex], LAST[ex]
        sent_i.append(Shift((1, 0, 0), intact.at[k0:k1, bx - ex :, :, :], B["ix"].at[k0:k1, 0:ex, own, :]))

    shift_main("u")

    def prepare(x, carry):
        for k in ORDER:
            ex, ey, ez = OFFSETS[k]
            factor = jnp.where(x + ex < bx, terms(k)[0], 0.0) if ex else terms(k)[0]
            B["jf"][k, x] = intact[k, x].astype(jnp.float32) * mask(ey, ez) * factor
        return carry

    lax.fori_loop(0, bx, prepare, 0)

    y_planes = {}
    for ex in range(H + 1):
        y_planes[ex] = jnp.where(row + ex < bx, 1.0, beyond_x)

    def own_flags(e):
        kind, at, step = e
        k, mine = bond_of(step)
        if kind == "x":
            return intact[k, at].astype(jnp.float32) * mask(*step[1:]) * (terms(k)[0] * beyond_x)
        value = intact_flat[k, pl.ds(at, bx, stride=by), :].astype(jnp.float32) * B["lanes"][step[2] + H]
        return value * (y_planes[step[0]] * (terms(k)[0] * number(has["gy", 1 if step[1] > 0 else -1])))

    for e in x_list + y_list:
        if bond_of(e[2])[1]:
            B["hj"][place[e]] = own_flags(e)

    def length(d, k):
        long2 = d[0] * d[0] + d[1] * d[1] + d[2] * d[2]
        return long2, long2 * lax.rsqrt(long2) - radius_of(k)

    acc_t, acc_f = B["t", "sums"], B["u", "sums"]
    uz, tz = B["u", "main"], B["t", "main"]

    def dilate(x, carry):
        mine = [u[c, x + H, own, :] for c in range(3)]
        near = [{v: mine[c] - float(v) if v else mine[c] for v in range(-H, H + 1)} for c in range(3)]
        total = zero
        for k in ORDER:
            ex, ey, ez = OFFSETS[k]
            part = slice(PAD + ey, PAD + ey + by)
            d = [uz[ez + H, c, x + ex, part, :] - near[c][OFFSETS[k][c]] for c in range(3)]
            long2, ext = length(d, k)
            term = B["jf"][k, x] * ext
            for c in range(3):
                B["d"][k, x, c] = d[c]
            B["ext"][k, x] = ext
            B["len"][k, x] = long2
            total = total + term
            acc_t[ez + H, x + ex, 0, part, :] += term
        B["t", "base"][0, x] = total
        return carry

    lax.fori_loop(0, bx, dilate, 0)

    def gather(name):
        sums, base = B[name, "sums"], B[name, "base"]
        for c in range(base.shape[0]):

            def body(x, carry, c=c):
                value = base[c, x] + sums[H, x, c, own, :]
                for ez in (-3, -2, -1, 1, 2, 3):
                    value = value + roll(sums[ez + H, x, c, own, :], ez) * B["lanes"][H - ez]
                base[c, x] = value
                return carry

            lax.fori_loop(0, bx, body, 0)

    gather("t")

    def soften_one(j, ext, long2, k):
        _, p, q = terms(k)
        more = 1.0 + (ext * ext) * (1.0 / (radius_of(k) * soft_stretch) ** 2)
        scale = j * lax.rsqrt(more * more * long2)
        return scale * p, scale * ext * q

    def soften(x, carry):
        for k in ORDER:
            B["len"][k, x], B["ext"][k, x] = soften_one(B["jf"][k, x], B["ext"][k, x], B["len"][k, x], k)
        return carry

    lax.fori_loop(0, bx, soften, 0)

    def beside(name):
        field, z = B[name, "field"], B[name, "z"]
        field_flat = u_flat if name == "u" else t_flat
        comps = field.shape[0]
        for c in range(comps):
            for i in range(2 * H):
                plane = i if i < H else i + bx
                value = field[c, plane, own, :]
                for ez in range(-H, H + 1):
                    B[name, "x"][ez + H, c, i, own, :] = roll(value, -ez)
                at = PAD - H + i if i < H else PAD + by + i - H
                for half in range(2):
                    value = field_flat[c, pl.ds(half * bx * rows + at, bx, stride=rows), :]
                    for ez in range(-H, H + 1):
                        B[name, "y"][ez + H, c, i, half * bx : half * bx + bx, :] = roll(value, -ez)
            for tile in (slice(0, by), slice(by, rows)):
                near, left, right = [jnp.where(high, z[0, i, c, tile, :], z[1, i, c, tile, :]) for i in (1, 0, 2)]
                far = roll(jnp.where(lane < bz // 2 - GROUP, right, left), bx * GROUP)
                value = jnp.where(inner, near, far)
                for i, (ex, az) in enumerate(MOVES):
                    over = roll(value, GROUP - GROUP * ex - az)
                    under = roll(value, -GROUP - GROUP * ex + az)
                    B[name, "q"][i, c, tile, :] = jnp.where(high, over, under)

    for copy in sent_u:
        copy.receive()
    beside("u")

    strip_sign = jnp.where(high, 1.0, -1.0)

    def other(name, e, c):
        kind, at, (ex, ey, ez) = e
        if kind == "x":
            i = at + ex + H if at + ex < 0 else at + ex - bx + H
            return B[name, "x"][ez + H, c, i, PAD + ey : PAD + ey + by, :]
        if kind == "y":
            i = at + ey + H if at + ey < 0 else at + ey - by + H
            return B[name, "y"][ez + H, c, i, H + ex : H + ex + bx, :]
        return B[name, "q"][MOVES.index((ex, ez)), c, PAD + ey : PAD + ey + by, :]

    def inside(name, kind, at, c):
        if kind == "x":
            return B[name, "field"][c, at + H, own, :]
        if kind == "y":
            flat_field = u_flat if name == "u" else t_flat
            return flat_field[c, pl.ds(H * rows + PAD + at, bx, stride=rows), :]
        return B[name, "in"][c]

    def bond(e):
        return NUMBER[e[2]] if e[0] == "z" and e[2] in NUMBER else bond_of(e[2])[0]

    def stretch(part, total):
        near, was = {}, None
        for e in part:
            kind, at, step = e
            if (kind, at) != was:
                was, near = (kind, at), {}
            i, k = place[e], bond(e)
            d = []
            for c in range(3):
                if (c, step[c]) not in near:
                    if (c, None) not in near:
                        near[c, None] = inside("u", kind, at, c)
                    start = near[c, None]
                    if step[c]:
                        move = strip_sign * float(step[c]) if kind == "z" and c == 2 else float(step[c])
                        start = start - move
                    near[c, step[c]] = start
                d.append(other("u", e, c) - near[c, step[c]])
            long2, ext = length(d, k)
            for c in range(3):
                B["hd"][i, c] = d[c]
            B["hext"][i] = ext
            B["hlen"][i] = long2
            term = B["hj"][i] * ext
            total[kind, at] = total[kind, at] + term if (kind, at) in total else term

    def from_slots(ex, ey, az):
        got, s = B["slots"], SLOT[ex, ey, az]
        part = slice(PAD - ey, PAD - ey + by)
        value = jnp.where(high, got[0, 0, s, part, :], got[1, 0, s, part, :])
        if ex:
            far = jnp.where(high, got[0, 1, s, part, :], got[1, 1, s, part, :])
            value = jnp.where(inner, value, roll(far, bx * GROUP))
        over = roll(value, GROUP + GROUP * ex - az)
        under = roll(value, -GROUP + GROUP * ex + az)
        return jnp.where(spot >= GROUP - az, over, jnp.where(spot < az, under, 0.0))

    def taken_flags(e):
        kind, at, step = e
        ex, ey, ez = minus(step)
        k = NUMBER[ex, ey, ez]
        if kind == "x":
            value = B["ix"][k, at, PAD - ey : PAD - ey + by, :].astype(jnp.float32)
            return roll(value, ez) * (mask(*step[1:]) * terms(k)[0])
        from_row = at - ey + by if ey > 0 else at - ey - by
        value = iy_flat[k, pl.ds(from_row, bx, stride=by), :].astype(jnp.float32)
        return roll(value, ez) * (B["lanes"][step[2] + H] * terms(k)[0])

    sums_t = {}
    stretch([e for e in x_list + y_list if bond_of(e[2])[1]], sums_t)
    for copy in sent_i:
        copy.receive()
    for e in x_list + y_list:
        if not bond_of(e[2])[1]:
            B["hj"][place[e]] = taken_flags(e)
    for e in z_list:
        ex, ey, az = e[2]
        value = B["own_slots"][SLOT[e[2]]] if e[2] in SLOT else None
        if (-ex, -ey, az) in SLOT:
            more = from_slots(-ex, -ey, az)
            value = more if value is None else value + more
        B["hj"][place[e]] = value
    stretch([e for e in x_list + y_list if not bond_of(e[2])[1]], sums_t)
    stretch(z_list, sums_t)

    def finish(name, c, total, write):
        base = B[name, "base"]
        base_flat = flat(base)
        for r in range(by):
            if ("y", r) in total:
                base_flat[c, pl.ds(r, bx, stride=by), :] += total["y", r]
        for x, strip in enumerate(unpack(total["z", 0])):
            value = base[c, x] + strip
            if ("x", x) in total:
                value = value + total["x", x]
            write(x, value)

    t = B["t", "field"]
    own_theta = []

    def write_theta(x, value):
        theta_out[x] = value
        t[0, x + H, own, :] = value
        own_theta.append(value)

    finish("t", 0, sums_t, write_theta)
    B["t", "in"][0] = pack(own_theta)
    sent_t = spread("t")

    shift_main("t")

    def push(x, carry):
        here = t[0, x + H, own, :]
        total = [zero, zero, zero]
        for k in ORDER:
            ex, ey, ez = OFFSETS[k]
            part = slice(PAD + ey, PAD + ey + by)
            scalar = B["len"][k, x] * (here + tz[ez + H, 0, x + ex, part, :]) + B["ext"][k, x]
            for c in range(3):
                pushed = scalar * B["d"][k, x, c]
                total[c] = total[c] + pushed
                acc_f[ez + H, x + ex, c, part, :] -= pushed
        for c in range(3):
            B["u", "base"][c, x] = total[c]
        return carry

    lax.fori_loop(0, bx, push, 0)
    gather("u")
    for e in everything:
        i = place[e]
        B["hlen"][i], B["hext"][i] = soften_one(B["hj"][i], B["hext"][i], B["hlen"][i], bond(e))

    for copy in sent_t:
        copy.receive()
    beside("t")
    sums_f = [{}, {}, {}]
    for e in everything:
        kind, at, _ = e
        i = place[e]
        scalar = B["hlen"][i] * (inside("t", kind, at, 0) + other("t", e, 0)) + B["hext"][i]
        for c in range(3):
            pushed = scalar * B["hd"][i, c]
            total = sums_f[c]
            total[kind, at] = total[kind, at] + pushed if (kind, at) in total else pushed

    for c in range(3):

        def write_force(x, value, c=c):
            force_out[c, x] = value

        finish("u", c, sums_f[c], write_force)
    for copy in copies:
        copy.finish()


def shards(sizes, displacement, bond_intact):
    plan = scratch_plan(bond_intact.shape[0], *displacement.shape[1:])
    scratch = [pltpu.VMEM(shape, dtype) for dtype, shape in plan.values()]
    scratch += [
        pltpu.VMEM(bond_intact.shape, jnp.int32),
        pltpu.SemaphoreType.DMA((96,)),
        pltpu.SemaphoreType.DMA((96,)),
        pltpu.SemaphoreType.DMA((2,)),
    ]
    vmem, anywhere = pl.BlockSpec(memory_space=pltpu.VMEM), pl.BlockSpec(memory_space=pl.ANY)
    return pl.pallas_call(
        functools.partial(kernel, sizes, tuple(plan)),
        out_shape=(
            jax.ShapeDtypeStruct(displacement.shape, jnp.float32),
            jax.ShapeDtypeStruct(displacement.shape[1:], jnp.float32),
        ),
        in_specs=[anywhere, anywhere],
        out_specs=(vmem, vmem),
        scratch_shapes=scratch,
        compiler_params=pltpu.CompilerParams(collective_id=0, has_side_effects=True, vmem_limit_bytes=62000000),
    )(displacement, bond_intact)


def solution(mesh):
    sizes = {a: mesh.shape[a] for a in AXES}
    return jax.shard_map(
        functools.partial(shards, sizes),
        mesh=mesh,
        in_specs=(P(None, "gx", "gy", "gz"), P(None, "gx", "gy", "gz")),
        out_specs=(P(None, "gx", "gy", "gz"), P("gx", "gy", "gz")),
        check_vma=False,
    )
```

```python
import functools
import math

import jax
import jax.numpy as jnp
from jax import lax
from jax.experimental import pallas as pl
from jax.experimental.pallas import tpu as pltpu
from jax.sharding import PartitionSpec as P

MESH = pl.DeviceIdType.MESH
bulk_modulus = 150.0
shear_modulus = 25.0
soft_stretch = 0.05
AXES = ("gx", "gy", "gz")
H = 3
PAD = 4
GROUP = 8


def bond_offsets():
    chosen = []
    for step_x in range(0, 4):
        for step_y in range(-3, 4):
            for step_z in range(-3, 4):
                if step_x * step_x + step_y * step_y + step_z * step_z > 9:
                    continue
                if step_x > 0 or (step_x == 0 and (step_y > 0 or (step_y == 0 and step_z > 0))):
                    chosen.append((step_x, step_y, step_z))
    return chosen


OFFSETS = bond_offsets()
NUMBER = {o: k for k, o in enumerate(OFFSETS)}
ORDER = sorted(range(len(OFFSETS)), key=lambda k: (OFFSETS[k][:2], OFFSETS[k][2]))


def square(offset):
    return sum(step * step for step in offset)


VOLUME = 2.0 * sum(math.exp(-square(o) / 9.0) * square(o) for o in OFFSETS)


def minus(offset):
    return tuple(-step for step in offset)


def bond_of(step):
    return (NUMBER[step], True) if step in NUMBER else (NUMBER[minus(step)], False)


def radius_of(k):
    return math.sqrt(square(OFFSETS[k]))


def terms(k):
    weight, radius = math.exp(-square(OFFSETS[k]) / 9.0), radius_of(k)
    c = 3.0 / VOLUME * weight * radius
    a = 3.0 * bulk_modulus / VOLUME * weight * radius
    b = 15.0 * shear_modulus / VOLUME * weight
    return c, (a - b * radius / 3.0) / c, 2.0 * b / c


STEPS = [s for o in OFFSETS for s in (o, minus(o))]
PAIRS = sorted({s[1:] for s in STEPS})
FIRST = {}
LAST = {}
for _k, _o in enumerate(OFFSETS):
    FIRST.setdefault(_o[0], _k)
    LAST[_o[0]] = _k + 1
RUNS = {}
for _k, _o in enumerate(OFFSETS):
    if _o[1]:
        RUNS.setdefault(_o[:2], []).append(_k)
RUNS = {g: (ks[0], ks[-1] + 1) for g, ks in RUNS.items()}

SLOTS = sorted(
    {(o[0], o[1], abs(o[2])) for o in OFFSETS if o[2]},
    key=lambda s: ((0 if s[1] > 0 else 1 if s[1] < 0 else 2), s[0] if s[1] else -s[0], s),
)
SLOT = {s: i for i, s in enumerate(SLOTS)}
STRIP = sorted({(s[0], s[1], abs(s[2])) for s in STEPS if s[2]})
MOVES = sorted({(s[0], s[2]) for s in STRIP})


def span(test):
    found = [i for i, s in enumerate(SLOTS) if test(s)]
    assert found == list(range(found[0], found[-1] + 1))
    return slice(found[0], found[-1] + 1)


def side(step, size, at):
    return slice(at - H, at) if step < 0 else slice(at + size, at + size + H) if step > 0 else slice(at, at + size)


def edge_of(step, size, at):
    return slice(at, at + H) if step < 0 else slice(at + size - H, at + size) if step > 0 else slice(at, at + size)


def evaluations(bx, by):
    x_list, y_list = [], []
    for x in range(bx):
        x_list += [("x", x, s) for s in sorted(STEPS, key=lambda s: (s[1], s[2])) if not 0 <= x + s[0] < bx]
    for r in range(by):
        y_list += [("y", r, s) for s in sorted(STEPS, key=lambda s: (s[0], s[2])) if not 0 <= r + s[1] < by]
    return x_list, y_list, [("z", 0, s) for s in STRIP]


def scratch_plan(bonds, bx, by, bz):
    rows, planes, f, i = by + 2 * PAD, 2 * bx, jnp.float32, jnp.int32
    halo = sum(len(part) for part in evaluations(bx, by))
    plan = {"jf": (f, (bonds, bx, by, bz)), "ext": (f, (bonds, bx, by, bz)), "len": (f, (bonds, bx, by, bz))}
    plan["d"] = (f, (bonds, bx, 3, by, bz))
    plan["hj"] = plan["hext"] = plan["hlen"] = (f, (halo, by, bz))
    plan["hd"] = (f, (halo, 3, by, bz))
    plan["mask"] = (f, (len(PAIRS), by, bz))
    plan["lanes"] = (f, (7, by, bz))
    plan["ix"] = (i, (bonds, H, rows, bz))
    plan["iy"] = (i, (bonds, bx, by, bz))
    plan["own_slots"] = (f, (len(SLOTS), by, bz))
    plan["slots"] = (f, (2, 2, len(SLOTS), rows, bz))
    for name, c in (("u", 3), ("t", 1)):
        plan[name, "field"] = (f, (c, planes, rows, bz))
        plan[name, "main"] = (f, (7, c, bx + H, rows, bz))
        plan[name, "sums"] = (f, (7, bx + H, c, rows, bz))
        plan[name, "base"] = (f, (c, bx, by, bz))
        plan[name, "x"] = (f, (7, c, 2 * H, rows, bz))
        plan[name, "y"] = (f, (7, c, 2 * H, planes, bz))
        plan[name, "in"] = (f, (c, by, bz))
        plan[name, "z"] = (f, (2, 3, c, rows, bz))
        plan[name, "q"] = (f, (len(MOVES), c, rows, bz))
    return plan


def kernel(sizes, names, u_hbm, intact_hbm, force_out, theta_out, *scratch):
    B = dict(zip(names, scratch))
    intact, send_sem, recv_sem, load_sem = scratch[len(names) :]
    bx, by, bz = theta_out.shape
    rows, planes = by + 2 * PAD, 2 * bx
    assert bx == by and planes * GROUP == bz and GROUP >= 2 * H + 2
    x_list, y_list, z_list = evaluations(bx, by)
    everything = x_list + y_list + z_list
    place = {e: i for i, e in enumerate(everything)}
    index = {a: lax.axis_index(a) for a in AXES}
    has = {(a, -1): index[a] > 0 for a in AXES}
    has.update({(a, 1): index[a] < sizes[a] - 1 for a in AXES})
    own = slice(PAD, PAD + by)

    def there(direction):
        found = None
        for a, step in zip(AXES, direction):
            if step:
                found = has[a, step] if found is None else found & has[a, step]
        return found

    everyone = [(x, y, z) for x in (-1, 0, 1) for y in (-1, 0, 1) for z in (-1, 0, 1) if x or y or z]
    exists = {d: there(d) for d in everyone}

    def device(direction):
        return {a: index[a] + step for a, step in zip(AXES, direction) if step}

    u = B["u", "field"]
    load_u = pltpu.make_async_copy(u_hbm, u.at[:, H : H + bx, own, :], load_sem.at[0])
    load_u.start()
    load = pltpu.make_async_copy(intact_hbm, intact, load_sem.at[1])
    load.start()

    barrier = pltpu.get_barrier_semaphore()
    count = jnp.int32(0)
    for d in everyone:
        count = count + jnp.where(exists[d], 1, 0).astype(jnp.int32)

        @pl.when(exists[d])
        def _(d=d):
            pl.semaphore_signal(barrier, inc=1, device_id=device(d), device_id_type=MESH)

    copies = []

    class Shift:
        def __init__(self, direction, src, dst):
            number = len(copies)
            copies.append(self)
            self.direction = direction
            self.copy = pltpu.make_async_remote_copy(
                src_ref=src, dst_ref=dst, send_sem=send_sem.at[number], recv_sem=recv_sem.at[number],
                device_id=device(direction), device_id_type=MESH,
            )
            self.sends = exists[direction]
            self.takes = exists[minus(direction)]

            @pl.when(self.sends)
            def _():
                self.copy.start()

        def receive(self):
            @pl.when(self.takes)
            def _():
                self.copy.wait_recv()

        def finish(self):
            @pl.when(self.sends)
            def _():
                self.copy.wait_send()

    def nothing(view):
        view[...] = jnp.zeros(view.shape, view.dtype)

    def landing(name, d):
        if d[2]:
            return B[name, "z"].at[(d[2] + 1) // 2, d[0] + 1, :, side(d[1], by, PAD), :]
        return B[name, "field"].at[:, side(d[0], bx, H), side(d[1], by, PAD), :]

    SENT = (slice(0, by), slice(by - 2, by), slice(0, 2))
    LAND = (slice(PAD, PAD + by), slice(PAD - 2, PAD), slice(PAD + by, PAD + by + 2))
    up, down = span(lambda s: s[1] > 0), span(lambda s: s[1] < 0)
    x_all, x_up = span(lambda s: s[0] > 0), span(lambda s: s[0] > 0 and s[1] > 0)
    slot_moves = []
    for dz in (-1, 1):
        for dx, parts in ((0, (slice(0, len(SLOTS)), up, down)), (1, (x_all, x_up, down))):
            for way, dy in enumerate((0, 1, -1)):
                slot_moves.append(((dx, dy, dz), parts[way], way))

    def slot_landing(d, part, way):
        return B["slots"].at[(1 - d[2]) // 2, d[0], part, LAND[way], :]

    lane = lax.broadcasted_iota(jnp.int32, (by, bz), 1)
    row = lax.broadcasted_iota(jnp.int32, (by, bz), 0)
    spot = lax.rem(lane, GROUP)
    high = spot >= GROUP // 2
    edge = (lane < H) | (lane >= bz - H)
    inner = (lane >= H * GROUP) & (lane < (H + bx) * GROUP)
    zero = jnp.zeros((by, bz), jnp.float32)

    def number(condition):
        return jnp.where(condition, 1.0, 0.0)

    def roll(value, amount):
        return pltpu.roll(value, amount % bz, 1) if amount % bz else value

    def to_strip(total):
        return jnp.where(high, roll(total, GROUP), total)

    def pack(tiles):
        total = zero
        for x, tile in enumerate(tiles):
            total = total + roll(jnp.where(edge, tile, 0.0), GROUP * (x + H))
        return to_strip(total)

    def unpack(strip):
        strip = jnp.where(high, roll(strip, -GROUP), strip)
        return [jnp.where(edge, roll(strip, -GROUP * (x + H)), 0.0) for x in range(bx)]

    def flat(ref, *at):
        return ref.reshape(*ref.shape[:-3], ref.shape[-3] * ref.shape[-2], bz)

    u_flat, t_flat, intact_flat = flat(u), flat(B["t", "field"]), flat(intact)
    iy_flat = flat(B["iy"])

    def clear(ref, depth):
        zeros = jnp.zeros(ref.shape[2:], jnp.float32)

        def body(i, carry):
            for s in range(depth):
                ref[s, i] = zeros
            return carry

        lax.fori_loop(0, ref.shape[1], body, 0)

    def mask(ey, ez):
        return B["mask"][PAIRS.index((ey, ez))]

    def shift_main(name):
        field, out = B[name, "field"], B[name, "main"]
        for c in range(field.shape[0]):

            def body(x, carry, c=c):
                value = field[c, x + H, own, :]
                for ez in range(1 - H, H + 1):
                    moved = roll(value, -ez)
                    out[ez + H, c, x, own, :] = moved
                    out[ez + H, c, x, 0:PAD, :] = moved[0:PAD]
                    out[ez + H, c, x, PAD + by :, :] = moved[0:PAD]
                return carry

            lax.fori_loop(0, bx, body, 0)

    load_u.wait()
    for c in range(3):
        B["u", "in"][c] = pack([u[c, x + H, own, :] for x in range(bx)])
    pl.semaphore_wait(barrier, count)

    def spread(name):
        field, strip = B[name, "field"], B[name, "in"]
        sent = []
        for d in sorted(everyone, key=lambda d: -sum(map(abs, d))):
            if d[2]:
                src = strip.at[:, edge_of(d[1], by, 0), :]
            else:
                src = field.at[:, edge_of(d[0], bx, H), edge_of(d[1], by, PAD), :]
            sent.append(Shift(d, src, landing(name, minus(d))))
        return sent

    sent_u = spread("u")
    load.wait()
    sent_i = []
    for (ex, ey), (k0, k1) in RUNS.items():
        toward = 1 if ey > 0 else -1
        at = slice(by - ey, by) if ey > 0 else slice(0, -ey)
        sent_i.append(
            Shift((0, toward, 0), intact.at[k0:k1, 0 : bx - ex, at, :], B["iy"].at[k0:k1, ex:, at, :])
        )
        if ex:
            sent_i.append(
                Shift((1, toward, 0), intact.at[k0:k1, bx - ex :, at, :], B["iy"].at[k0:k1, 0:ex, at, :])
            )
    for ex in range(1, H + 1):
        k0, k1 = FIRST[ex], LAST[ex]
        sent_i.append(Shift((1, 0, 0), intact.at[k0:k1, bx - ex :, :, :], B["ix"].at[k0:k1, 0:ex, own, :]))

    beyond_x = number(has["gx", 1])
    z_up, z_down = number(has["gz", 1]), number(has["gz", -1])

    def slots_body(x, totals):
        new = []
        crossing = jnp.where(has["gx", 1], 1.0, 0.0)
        for (ex, ey, az), total in zip(SLOTS, totals):
            value = jnp.where(lane >= bz - az, intact[NUMBER[ex, ey, az], x].astype(jnp.float32) * z_up, 0.0)
            if (ex, ey, -az) in NUMBER:
                other = intact[NUMBER[ex, ey, -az], x].astype(jnp.float32) * z_down
                value = jnp.where(lane < az, other, value)
            if ex:
                value = value * jnp.where(x + ex < bx, 1.0, crossing)
            new.append(total + pltpu.roll(value, GROUP * (x + H), 1))
        return tuple(new)

    totals = lax.fori_loop(0, bx, slots_body, tuple(zero for _ in SLOTS))
    y_inside = {}
    for ey in range(-H, H + 1):
        inside = (row + ey >= 0) & (row + ey < by)
        y_inside[ey] = jnp.where(inside, 1.0, number(has["gy", 1 if ey > 0 else -1])) if ey else None
    for (ex, ey, az), total in zip(SLOTS, totals):
        value = to_strip(total) * terms(NUMBER[ex, ey, az])[0]
        B["own_slots"][SLOT[ex, ey, az]] = value * y_inside[ey] if ey else value

    for e, part, way in reversed(slot_moves):
        sent_i.append(Shift(e, B["own_slots"].at[part, SENT[way], :], slot_landing(e, part, way)))

    for d in everyone:

        @pl.when(jnp.logical_not(exists[d]))
        def _(d=d):
            for name in ("u", "t"):
                nothing(landing(name, d))
            for e, part, way in slot_moves:
                if minus(e) == d:
                    nothing(slot_landing(e, part, way))
            if d == (-1, 0, 0):
                nothing(B["ix"])
            for (ex, ey), (k0, k1) in RUNS.items():
                back = -1 if ey > 0 else 1
                at = slice(by - ey, by) if ey > 0 else slice(0, -ey)
                if d == (0, back, 0):
                    nothing(B["iy"].at[k0:k1, ex:, at, :])
                if ex and d == (-1, back, 0):
                    nothing(B["iy"].at[k0:k1, 0:ex, at, :])

    for i, (ey, ez) in enumerate(PAIRS):
        B["mask"][i] = number((row + ey >= 0) & (row + ey < by) & (lane + ez >= 0) & (lane + ez < bz))
    for ez in range(-H, H + 1):
        B["lanes"][ez + H] = number((lane + ez >= 0) & (lane + ez < bz))

    def blank_rows(i, carry):
        for name in ("u", "t"):
            out = B[name, "x"]
            for c in range(out.shape[1]):
                for s in range(7):
                    for part in (slice(0, PAD), slice(PAD + by, rows)):
                        out[s, c, i, part, :] = jnp.zeros((PAD, bz), jnp.float32)
        return carry

    lax.fori_loop(0, 2 * H, blank_rows, 0)

    def blank_planes(i, carry):
        for name in ("u", "t"):
            out = B[name, "main"]
            for c in range(out.shape[1]):
                for s in range(7):
                    out[s, c, i] = jnp.zeros((rows, bz), jnp.float32)
        return carry

    lax.fori_loop(bx, bx + H, blank_planes, 0)
    clear(B["t", "sums"], 7)
    clear(B["u", "sums"], 7)

    shift_main("u")

    def prepare(x, carry):
        for k in ORDER:
            ex, ey, ez = OFFSETS[k]
            factor = jnp.where(x + ex < bx, terms(k)[0], 0.0) if ex else terms(k)[0]
            B["jf"][k, x] = intact[k, x].astype(jnp.float32) * mask(ey, ez) * factor
        return carry

    lax.fori_loop(0, bx, prepare, 0)

    y_planes = {}
    for ex in range(H + 1):
        y_planes[ex] = jnp.where(row + ex < bx, 1.0, beyond_x)

    def own_flags(e):
        kind, at, step = e
        k, mine = bond_of(step)
        if kind == "x":
            return intact[k, at].astype(jnp.float32) * mask(*step[1:]) * (terms(k)[0] * beyond_x)
        value = intact_flat[k, pl.ds(at, bx, stride=by), :].astype(jnp.float32) * B["lanes"][step[2] + H]
        return value * (y_planes[step[0]] * (terms(k)[0] * number(has["gy", 1 if step[1] > 0 else -1])))

    for e in x_list + y_list:
        if bond_of(e[2])[1]:
            B["hj"][place[e]] = own_flags(e)

    def length(d, k):
        long2 = d[0] * d[0] + d[1] * d[1] + d[2] * d[2]
        return long2, long2 * lax.rsqrt(long2) - radius_of(k)

    acc_t, acc_f = B["t", "sums"], B["u", "sums"]
    uz, tz = B["u", "main"], B["t", "main"]

    def dilate(x, carry):
        mine = [u[c, x + H, own, :] for c in range(3)]
        near = [{v: mine[c] - float(v) if v else mine[c] for v in range(-H, H + 1)} for c in range(3)]
        total = zero
        for k in ORDER:
            ex, ey, ez = OFFSETS[k]
            part = slice(PAD + ey, PAD + ey + by)
            d = [uz[ez + H, c, x + ex, part, :] - near[c][OFFSETS[k][c]] for c in range(3)]
            long2, ext = length(d, k)
            term = B["jf"][k, x] * ext
            for c in range(3):
                B["d"][k, x, c] = d[c]
            B["ext"][k, x] = ext
            B["len"][k, x] = long2
            total = total + term
            acc_t[ez + H, x + ex, 0, part, :] += term
        B["t", "base"][0, x] = total
        return carry

    lax.fori_loop(0, bx, dilate, 0)

    def gather(name):
        sums, base = B[name, "sums"], B[name, "base"]
        for c in range(base.shape[0]):

            def body(x, carry, c=c):
                value = base[c, x] + sums[H, x, c, own, :]
                for ez in (-3, -2, -1, 1, 2, 3):
                    value = value + roll(sums[ez + H, x, c, own, :], ez) * B["lanes"][H - ez]
                base[c, x] = value
                return carry

            lax.fori_loop(0, bx, body, 0)

    gather("t")

    def soften_one(j, ext, long2, k):
        _, p, q = terms(k)
        more = 1.0 + (ext * ext) * (1.0 / (radius_of(k) * soft_stretch) ** 2)
        scale = j * lax.rsqrt(more * more * long2)
        return scale * p, scale * ext * q

    NEEDED = (0, 2, 2, 2, 2, 0)

    def beside_x(name):
        field, out = B[name, "field"], B[name, "x"]
        for c in range(field.shape[0]):
            for i in range(2 * H):
                value = field[c, i if i < H else i + bx, own, :]
                for ez in range(-NEEDED[i], NEEDED[i] + 1):
                    out[ez + H, c, i, own, :] = roll(value, -ez)

    def beside_y(name):
        field_flat, out = flat(B[name, "field"]), B[name, "y"]
        for c in range(out.shape[1]):
            for i in range(2 * H):
                at = PAD - H + i if i < H else PAD + by + i - H
                for half in range(2):
                    value = field_flat[c, pl.ds(half * bx * rows + at, bx, stride=rows), :]
                    for ez in range(-NEEDED[i], NEEDED[i] + 1):
                        out[ez + H, c, i, half * bx : half * bx + bx, :] = roll(value, -ez)

    def beside_z(name):
        z, out = B[name, "z"], B[name, "q"]
        for c in range(out.shape[1]):
            for tile in (slice(0, by), slice(by, rows)):
                near, left, right = [jnp.where(high, z[0, i, c, tile, :], z[1, i, c, tile, :]) for i in (1, 0, 2)]
                far = roll(jnp.where(lane < bz // 2 - GROUP, right, left), bx * GROUP)
                value = jnp.where(inner, near, far)
                for i, (ex, az) in enumerate(MOVES):
                    over = roll(value, GROUP - GROUP * ex - az)
                    under = roll(value, -GROUP - GROUP * ex + az)
                    out[i, c, tile, :] = jnp.where(high, over, under)

    def receive(sent, kind):
        for copy in sent:
            dx, dy, dz = copy.direction
            if ("z" if dz else "y" if dy else "x") == kind:
                copy.receive()

    strip_sign = jnp.where(high, 1.0, -1.0)

    def other(name, e, c):
        kind, at, (ex, ey, ez) = e
        if kind == "x":
            i = at + ex + H if at + ex < 0 else at + ex - bx + H
            return B[name, "x"][ez + H, c, i, PAD + ey : PAD + ey + by, :]
        if kind == "y":
            i = at + ey + H if at + ey < 0 else at + ey - by + H
            return B[name, "y"][ez + H, c, i, H + ex : H + ex + bx, :]
        return B[name, "q"][MOVES.index((ex, ez)), c, PAD + ey : PAD + ey + by, :]

    def inside(name, kind, at, c):
        if kind == "x":
            return B[name, "field"][c, at + H, own, :]
        if kind == "y":
            flat_field = u_flat if name == "u" else t_flat
            return flat_field[c, pl.ds(H * rows + PAD + at, bx, stride=rows), :]
        return B[name, "in"][c]

    def bond(e):
        return NUMBER[e[2]] if e[0] == "z" and e[2] in NUMBER else bond_of(e[2])[0]

    def add(name, kind, at, totals):
        base = B[name, "base"]
        for c, total in enumerate(totals):
            if kind == "x":
                base[c, at] += total
            else:
                base_flat = flat(base)
                base_flat[c, pl.ds(at, bx, stride=by), :] += total

    def stretch(part):
        near, was, total = {}, None, None
        for e in part:
            kind, at, step = e
            if (kind, at) != was:
                if was is not None:
                    add("t", *was, [total])
                was, near, total = (kind, at), {}, None
            i, k = place[e], bond(e)
            d = []
            for c in range(3):
                if (c, step[c]) not in near:
                    if (c, None) not in near:
                        near[c, None] = inside("u", kind, at, c)
                    start = near[c, None]
                    if step[c]:
                        move = strip_sign * float(step[c]) if kind == "z" and c == 2 else float(step[c])
                        start = start - move
                    near[c, step[c]] = start
                d.append(other("u", e, c) - near[c, step[c]])
            long2, ext = length(d, k)
            for c in range(3):
                B["hd"][i, c] = d[c]
            B["hext"][i] = ext
            B["hlen"][i] = long2
            term = B["hj"][i] * ext
            total = total + term if total is not None else term
        if was[0] == "z":
            return total
        add("t", *was, [total])

    def from_slots(ex, ey, az):
        got, s = B["slots"], SLOT[ex, ey, az]
        part = slice(PAD - ey, PAD - ey + by)
        value = jnp.where(high, got[0, 0, s, part, :], got[1, 0, s, part, :])
        if ex:
            far = jnp.where(high, got[0, 1, s, part, :], got[1, 1, s, part, :])
            value = jnp.where(inner, value, roll(far, bx * GROUP))
        over = roll(value, GROUP + GROUP * ex - az)
        under = roll(value, -GROUP + GROUP * ex + az)
        return jnp.where(spot >= GROUP - az, over, jnp.where(spot < az, under, 0.0))

    def taken_flags(e):
        kind, at, step = e
        ex, ey, ez = minus(step)
        k = NUMBER[ex, ey, ez]
        if kind == "x":
            value = B["ix"][k, at, PAD - ey : PAD - ey + by, :].astype(jnp.float32)
            return roll(value, ez) * (mask(*step[1:]) * terms(k)[0])
        from_row = at - ey + by if ey > 0 else at - ey - by
        value = iy_flat[k, pl.ds(from_row, bx, stride=by), :].astype(jnp.float32)
        return roll(value, ez) * (B["lanes"][step[2] + H] * terms(k)[0])

    own_x, taken_x = [[e for e in x_list if bond_of(e[2])[1] == mine] for mine in (True, False)]
    own_y, taken_y = [[e for e in y_list if bond_of(e[2])[1] == mine] for mine in (True, False)]
    receive(sent_u, "x")
    beside_x("u")
    stretch(own_x)
    receive(sent_u, "y")
    beside_y("u")
    stretch(own_y)
    receive(sent_u, "z")
    beside_z("u")
    receive(sent_i, "x")
    for e in taken_x:
        B["hj"][place[e]] = taken_flags(e)
    stretch(taken_x)
    receive(sent_i, "z")
    for e in z_list:
        ex, ey, az = e[2]
        value = B["own_slots"][SLOT[e[2]]] if e[2] in SLOT else None
        if (-ex, -ey, az) in SLOT:
            more = from_slots(-ex, -ey, az)
            value = more if value is None else value + more
        B["hj"][place[e]] = value
    strip_t = stretch(z_list)
    receive(sent_i, "y")
    for e in taken_y:
        B["hj"][place[e]] = taken_flags(e)
    stretch(taken_y)

    def finish(name, c, strip, write):
        base = B[name, "base"]
        for x, part in enumerate(unpack(strip)):
            write(x, base[c, x] + part)

    t = B["t", "field"]
    own_theta = []

    def write_theta(x, value):
        theta_out[x] = value
        t[0, x + H, own, :] = value
        own_theta.append(value)

    finish("t", 0, strip_t, write_theta)
    B["t", "in"][0] = pack(own_theta)
    sent_t = spread("t")

    shift_main("t")

    def push(x, carry):
        here = t[0, x + H, own, :]
        total = [zero, zero, zero]
        for k in ORDER:
            ex, ey, ez = OFFSETS[k]
            part = slice(PAD + ey, PAD + ey + by)
            both, alone = soften_one(B["jf"][k, x], B["ext"][k, x], B["len"][k, x], k)
            scalar = both * (here + tz[ez + H, 0, x + ex, part, :]) + alone
            for c in range(3):
                pushed = scalar * B["d"][k, x, c]
                total[c] = total[c] + pushed
                acc_f[ez + H, x + ex, c, part, :] -= pushed
        for c in range(3):
            B["u", "base"][c, x] = total[c]
        return carry

    lax.fori_loop(0, bx, push, 0)
    gather("u")
    for e in everything:
        i = place[e]
        B["hlen"][i], B["hext"][i] = soften_one(B["hj"][i], B["hext"][i], B["hlen"][i], bond(e))

    for copy in copies:
        copy.finish()

    def forces(part):
        was, total = None, None
        for e in part:
            kind, at, _ = e
            if (kind, at) != was:
                if was is not None:
                    add("u", *was, total)
                was, total = (kind, at), None
                here = inside("t", kind, at, 0)
            i = place[e]
            scalar = B["hlen"][i] * (here + other("t", e, 0)) + B["hext"][i]
            pushed = [scalar * B["hd"][i, c] for c in range(3)]
            total = [total[c] + pushed[c] for c in range(3)] if total is not None else pushed
        if was[0] == "z":
            return total
        add("u", *was, total)

    receive(sent_t, "x")
    beside_x("t")
    forces(x_list)
    receive(sent_t, "y")
    beside_y("t")
    forces(y_list)
    receive(sent_t, "z")
    beside_z("t")
    strip_f = forces(z_list)

    for c in range(3):

        def write_force(x, value, c=c):
            force_out[c, x] = value

        finish("u", c, strip_f[c], write_force)


def shards(sizes, displacement, bond_intact):
    plan = scratch_plan(bond_intact.shape[0], *displacement.shape[1:])
    scratch = [pltpu.VMEM(shape, dtype) for dtype, shape in plan.values()]
    scratch += [
        pltpu.VMEM(bond_intact.shape, jnp.int32),
        pltpu.SemaphoreType.DMA((96,)),
        pltpu.SemaphoreType.DMA((96,)),
        pltpu.SemaphoreType.DMA((2,)),
    ]
    vmem, anywhere = pl.BlockSpec(memory_space=pltpu.VMEM), pl.BlockSpec(memory_space=pl.ANY)
    return pl.pallas_call(
        functools.partial(kernel, sizes, tuple(plan)),
        out_shape=(
            jax.ShapeDtypeStruct(displacement.shape, jnp.float32),
            jax.ShapeDtypeStruct(displacement.shape[1:], jnp.float32),
        ),
        in_specs=[anywhere, anywhere],
        out_specs=(vmem, vmem),
        scratch_shapes=scratch,
        compiler_params=pltpu.CompilerParams(collective_id=0, has_side_effects=True, vmem_limit_bytes=56375000),
    )(displacement, bond_intact)


def solution(mesh):
    sizes = {a: mesh.shape[a] for a in AXES}
    return jax.shard_map(
        functools.partial(shards, sizes),
        mesh=mesh,
        in_specs=(P(None, "gx", "gy", "gz"), P(None, "gx", "gy", "gz")),
        out_specs=(P(None, "gx", "gy", "gz"), P("gx", "gy", "gz")),
        check_vma=False,
    )
```

```python
import functools
import math

import jax
import jax.numpy as jnp
from jax import lax
from jax.experimental import pallas as pl
from jax.experimental.pallas import tpu as pltpu
from jax.sharding import PartitionSpec as P

MESH = pl.DeviceIdType.MESH
bulk_modulus = 150.0
shear_modulus = 25.0
soft_stretch = 0.05
AXES = ("gx", "gy", "gz")
H = 3
PAD = 4
GROUP = 8


def bond_offsets():
    chosen = []
    for step_x in range(0, 4):
        for step_y in range(-3, 4):
            for step_z in range(-3, 4):
                if step_x * step_x + step_y * step_y + step_z * step_z > 9:
                    continue
                if step_x > 0 or (step_x == 0 and (step_y > 0 or (step_y == 0 and step_z > 0))):
                    chosen.append((step_x, step_y, step_z))
    return chosen


OFFSETS = bond_offsets()
NUMBER = {o: k for k, o in enumerate(OFFSETS)}
ORDER = sorted(range(len(OFFSETS)), key=lambda k: (OFFSETS[k][:2], OFFSETS[k][2]))


def square(offset):
    return sum(step * step for step in offset)


VOLUME = 2.0 * sum(math.exp(-square(o) / 9.0) * square(o) for o in OFFSETS)


def minus(offset):
    return tuple(-step for step in offset)


def bond_of(step):
    return (NUMBER[step], True) if step in NUMBER else (NUMBER[minus(step)], False)


def radius_of(k):
    return math.sqrt(square(OFFSETS[k]))


def terms(k):
    weight, radius = math.exp(-square(OFFSETS[k]) / 9.0), radius_of(k)
    c = 3.0 / VOLUME * weight * radius
    a = 3.0 * bulk_modulus / VOLUME * weight * radius
    b = 15.0 * shear_modulus / VOLUME * weight
    return c, (a - b * radius / 3.0) / c, 2.0 * b / c


STEPS = [s for o in OFFSETS for s in (o, minus(o))]
PAIRS = sorted({s[1:] for s in STEPS})
FIRST = {}
LAST = {}
for _k, _o in enumerate(OFFSETS):
    FIRST.setdefault(_o[0], _k)
    LAST[_o[0]] = _k + 1
RUNS = {}
for _k, _o in enumerate(OFFSETS):
    if _o[1]:
        RUNS.setdefault(_o[:2], []).append(_k)
RUNS = {g: (ks[0], ks[-1] + 1) for g, ks in RUNS.items()}

SLOTS = sorted(
    {(o[0], o[1], abs(o[2])) for o in OFFSETS if o[2]},
    key=lambda s: ((0 if s[1] > 0 else 1 if s[1] < 0 else 2), s[0] if s[1] else -s[0], s),
)
SLOT = {s: i for i, s in enumerate(SLOTS)}
STRIP = sorted({(s[0], s[1], abs(s[2])) for s in STEPS if s[2]})
MOVES = sorted({(s[0], s[2]) for s in STRIP})


def span(test):
    found = [i for i, s in enumerate(SLOTS) if test(s)]
    assert found == list(range(found[0], found[-1] + 1))
    return slice(found[0], found[-1] + 1)


def side(step, size, at):
    return slice(at - H, at) if step < 0 else slice(at + size, at + size + H) if step > 0 else slice(at, at + size)


def edge_of(step, size, at):
    return slice(at, at + H) if step < 0 else slice(at + size - H, at + size) if step > 0 else slice(at, at + size)


def evaluations(bx, by):
    x_list, y_list = [], []
    for x in range(bx):
        x_list += [("x", x, s) for s in sorted(STEPS, key=lambda s: (s[1], s[2])) if not 0 <= x + s[0] < bx]
    for r in range(by):
        y_list += [("y", r, s) for s in sorted(STEPS, key=lambda s: (s[0], s[2])) if not 0 <= r + s[1] < by]
    return x_list, y_list, [("z", 0, s) for s in STRIP]


def scratch_plan(bonds, bx, by, bz):
    rows, planes, f, i = by + 2 * PAD, 2 * bx, jnp.float32, jnp.int32
    halo = sum(len(part) for part in evaluations(bx, by))
    plan = {"jf": (f, (bonds, bx, by, bz)), "ext": (f, (bonds, bx, by, bz)), "len": (f, (bonds, bx, by, bz))}
    plan["d"] = (f, (bonds, bx, 3, by, bz))
    plan["hj"] = plan["hext"] = plan["hlen"] = (f, (halo, by, bz))
    plan["hd"] = (f, (halo, 3, by, bz))
    plan["mask"] = (f, (len(PAIRS), by, bz))
    plan["lanes"] = (f, (7, by, bz))
    plan["scaled"] = (f, (bonds, by, bz))
    plan["ix"] = (i, (bonds, H, rows, bz))
    plan["iy"] = (i, (bonds, bx, by, bz))
    plan["own_slots"] = (f, (len(SLOTS), by, bz))
    plan["slots"] = (f, (2, 2, len(SLOTS), rows, bz))
    for name, c in (("u", 3), ("t", 1)):
        plan[name, "field"] = (f, (c, planes, rows, bz))
        plan[name, "main"] = (f, (7, c, bx, rows, bz))
        plan[name, "sums"] = (f, (7, bx, c, rows, bz))
        plan[name, "base"] = (f, (c, bx, by, bz))
        plan[name, "x"] = (f, (7, c, 2 * H, rows, bz))
        plan[name, "y"] = (f, (7, c, 2 * H, planes, bz))
        plan[name, "in"] = (f, (c, by, bz))
        plan[name, "z"] = (f, (2, 3, c, rows, bz))
        plan[name, "q"] = (f, (len(MOVES), c, rows, bz))
    return plan


def kernel(sizes, names, u_hbm, intact_hbm, force_out, theta_out, *scratch):
    B = dict(zip(names, scratch))
    intact, send_sem, recv_sem, load_sem = scratch[len(names) :]
    bx, by, bz = theta_out.shape
    rows, planes = by + 2 * PAD, 2 * bx
    assert bx == by and planes * GROUP == bz and GROUP >= 2 * H + 2
    x_list, y_list, z_list = evaluations(bx, by)
    everything = x_list + y_list + z_list
    place = {e: i for i, e in enumerate(everything)}
    index = {a: lax.axis_index(a) for a in AXES}
    has = {(a, -1): index[a] > 0 for a in AXES}
    has.update({(a, 1): index[a] < sizes[a] - 1 for a in AXES})
    own = slice(PAD, PAD + by)

    def there(direction):
        found = None
        for a, step in zip(AXES, direction):
            if step:
                found = has[a, step] if found is None else found & has[a, step]
        return found

    everyone = [(x, y, z) for x in (-1, 0, 1) for y in (-1, 0, 1) for z in (-1, 0, 1) if x or y or z]
    exists = {d: there(d) for d in everyone}

    def device(direction):
        return {a: index[a] + step for a, step in zip(AXES, direction) if step}

    u = B["u", "field"]
    load_u = pltpu.make_async_copy(u_hbm, u.at[:, H : H + bx, own, :], load_sem.at[0])
    load_u.start()
    load = pltpu.make_async_copy(intact_hbm, intact, load_sem.at[1])
    load.start()

    barrier = pltpu.get_barrier_semaphore()
    count = jnp.int32(0)
    for d in sorted(everyone, key=lambda d: -sum(map(abs, d))):
        count = count + jnp.where(exists[d], 1, 0).astype(jnp.int32)

        @pl.when(exists[d])
        def _(d=d):
            pl.semaphore_signal(barrier, inc=1, device_id=device(d), device_id_type=MESH)

    copies = []

    class Shift:
        def __init__(self, direction, src, dst):
            number = len(copies)
            copies.append(self)
            self.direction = direction
            self.copy = pltpu.make_async_remote_copy(
                src_ref=src, dst_ref=dst, send_sem=send_sem.at[number], recv_sem=recv_sem.at[number],
                device_id=device(direction), device_id_type=MESH,
            )
            self.sends = exists[direction]
            self.takes = exists[minus(direction)]

            @pl.when(self.sends)
            def _():
                self.copy.start()

        def receive(self):
            @pl.when(self.takes)
            def _():
                self.copy.wait_recv()

        def finish(self):
            @pl.when(self.sends)
            def _():
                self.copy.wait_send()

    def nothing(view):
        view[...] = jnp.zeros(view.shape, view.dtype)

    def landing(name, d):
        if d[2]:
            return B[name, "z"].at[(d[2] + 1) // 2, d[0] + 1, :, side(d[1], by, PAD), :]
        return B[name, "field"].at[:, side(d[0], bx, H), side(d[1], by, PAD), :]

    SENT = (slice(0, by), slice(by - 2, by), slice(0, 2))
    LAND = (slice(PAD, PAD + by), slice(PAD - 2, PAD), slice(PAD + by, PAD + by + 2))
    up, down = span(lambda s: s[1] > 0), span(lambda s: s[1] < 0)
    x_all, x_up = span(lambda s: s[0] > 0), span(lambda s: s[0] > 0 and s[1] > 0)
    slot_moves = []
    for dz in (-1, 1):
        for dx, parts in ((0, (slice(0, len(SLOTS)), up, down)), (1, (x_all, x_up, down))):
            for way, dy in enumerate((0, 1, -1)):
                slot_moves.append(((dx, dy, dz), parts[way], way))

    def slot_landing(d, part, way):
        return B["slots"].at[(1 - d[2]) // 2, d[0], part, LAND[way], :]

    lane = lax.broadcasted_iota(jnp.int32, (by, bz), 1)
    row = lax.broadcasted_iota(jnp.int32, (by, bz), 0)
    spot = lax.rem(lane, GROUP)
    high = spot >= GROUP // 2
    edge = (lane < H) | (lane >= bz - H)
    inner = (lane >= H * GROUP) & (lane < (H + bx) * GROUP)
    zero = jnp.zeros((by, bz), jnp.float32)

    def number(condition):
        return jnp.where(condition, 1.0, 0.0)

    def roll(value, amount):
        return pltpu.roll(value, amount % bz, 1) if amount % bz else value

    def to_strip(total):
        return jnp.where(high, roll(total, GROUP), total)

    def pack(tiles):
        total = zero
        for x, tile in enumerate(tiles):
            total = total + roll(jnp.where(edge, tile, 0.0), GROUP * (x + H))
        return to_strip(total)

    def unpack(strip):
        strip = jnp.where(high, roll(strip, -GROUP), strip)
        return [jnp.where(edge, roll(strip, -GROUP * (x + H)), 0.0) for x in range(bx)]

    def flat(ref, *at):
        return ref.reshape(*ref.shape[:-3], ref.shape[-3] * ref.shape[-2], bz)

    u_flat, t_flat, intact_flat = flat(u), flat(B["t", "field"]), flat(intact)
    iy_flat = flat(B["iy"])

    def clear(ref, depth):
        zeros = jnp.zeros(ref.shape[2:], jnp.float32)

        def body(i, carry):
            for s in range(1, depth):
                ref[s, i] = zeros
            return carry

        lax.fori_loop(0, ref.shape[1], body, 0)

    def mask(ey, ez):
        return B["mask"][PAIRS.index((ey, ez))]

    def shift_main(name):
        field, out = B[name, "field"], B[name, "main"]

        def body(x, carry):
            for c in range(field.shape[0]):
                value = field[c, x + H, own, :]
                for ez in range(1 - H, H + 1):
                    moved = roll(value, -ez)
                    out[ez + H, c, x, own, :] = moved
                    out[ez + H, c, x, 0:PAD, :] = moved[0:PAD]
                    out[ez + H, c, x, PAD + by :, :] = moved[0:PAD]
            return carry

        lax.fori_loop(0, bx, body, 0)

    for i, (ey, ez) in enumerate(PAIRS):
        B["mask"][i] = number((row + ey >= 0) & (row + ey < by) & (lane + ez >= 0) & (lane + ez < bz))
    for ez in range(-H, H + 1):
        B["lanes"][ez + H] = number((lane + ez >= 0) & (lane + ez < bz))

    def blank_rows(i, carry):
        for name in ("u", "t"):
            out = B[name, "x"]
            for c in range(out.shape[1]):
                for s in range(7):
                    for part in (slice(0, PAD), slice(PAD + by, rows)):
                        out[s, c, i, part, :] = jnp.zeros((PAD, bz), jnp.float32)
        return carry

    lax.fori_loop(0, 2 * H, blank_rows, 0)

    clear(B["t", "sums"], 7)
    clear(B["u", "sums"], 7)
    for k, (ex, ey, ez) in enumerate(OFFSETS):
        B["scaled"][k] = mask(ey, ez) * terms(k)[0]

    load_u.wait()
    for c in range(3):
        B["u", "in"][c] = pack([u[c, x + H, own, :] for x in range(bx)])
    shift_main("u")
    pl.semaphore_wait(barrier, count)

    def spread(name):
        field, strip = B[name, "field"], B[name, "in"]
        sent = []
        for d in sorted(everyone, key=lambda d: -sum(map(abs, d))):
            if d[2]:
                src = strip.at[:, edge_of(d[1], by, 0), :]
            else:
                src = field.at[:, edge_of(d[0], bx, H), edge_of(d[1], by, PAD), :]
            sent.append(Shift(d, src, landing(name, minus(d))))
        return sent

    sent_u = spread("u")
    load.wait()
    sent_i = []
    for (ex, ey), (k0, k1) in RUNS.items():
        toward = 1 if ey > 0 else -1
        at = slice(by - ey, by) if ey > 0 else slice(0, -ey)
        sent_i.append(
            Shift((0, toward, 0), intact.at[k0:k1, 0 : bx - ex, at, :], B["iy"].at[k0:k1, ex:, at, :])
        )
        if ex:
            sent_i.append(
                Shift((1, toward, 0), intact.at[k0:k1, bx - ex :, at, :], B["iy"].at[k0:k1, 0:ex, at, :])
            )
    for ex in range(1, H + 1):
        k0, k1 = FIRST[ex], LAST[ex]
        sent_i.append(Shift((1, 0, 0), intact.at[k0:k1, bx - ex :, :, :], B["ix"].at[k0:k1, 0:ex, own, :]))

    beyond_x = number(has["gx", 1])
    z_up, z_down = number(has["gz", 1]), number(has["gz", -1])

    def slots_body(x, totals):
        new = []
        crossing = jnp.where(has["gx", 1], 1.0, 0.0)
        for (ex, ey, az), total in zip(SLOTS, totals):
            value = jnp.where(lane >= bz - az, intact[NUMBER[ex, ey, az], x].astype(jnp.float32) * z_up, 0.0)
            if (ex, ey, -az) in NUMBER:
                other = intact[NUMBER[ex, ey, -az], x].astype(jnp.float32) * z_down
                value = jnp.where(lane < az, other, value)
            if ex:
                value = value * jnp.where(x + ex < bx, 1.0, crossing)
            new.append(total + pltpu.roll(value, GROUP * (x + H), 1))
        return tuple(new)

    totals = lax.fori_loop(0, bx, slots_body, tuple(zero for _ in SLOTS))
    y_inside = {}
    for ey in range(-H, H + 1):
        inside = (row + ey >= 0) & (row + ey < by)
        y_inside[ey] = jnp.where(inside, 1.0, number(has["gy", 1 if ey > 0 else -1])) if ey else None
    for (ex, ey, az), total in zip(SLOTS, totals):
        value = to_strip(total) * terms(NUMBER[ex, ey, az])[0]
        B["own_slots"][SLOT[ex, ey, az]] = value * y_inside[ey] if ey else value

    for e, part, way in reversed(slot_moves):
        sent_i.append(Shift(e, B["own_slots"].at[part, SENT[way], :], slot_landing(e, part, way)))

    for d in everyone:

        @pl.when(jnp.logical_not(exists[d]))
        def _(d=d):
            for name in ("u", "t"):
                nothing(landing(name, d))
            for e, part, way in slot_moves:
                if minus(e) == d:
                    nothing(slot_landing(e, part, way))
            if d == (-1, 0, 0):
                for ex in range(1, H + 1):
                    nothing(B["ix"].at[FIRST[ex] : LAST[ex], 0:ex, own, :])
            for (ex, ey), (k0, k1) in RUNS.items():
                back = -1 if ey > 0 else 1
                at = slice(by - ey, by) if ey > 0 else slice(0, -ey)
                if d == (0, back, 0):
                    nothing(B["iy"].at[k0:k1, ex:, at, :])
                if ex and d == (-1, back, 0):
                    nothing(B["iy"].at[k0:k1, 0:ex, at, :])


    y_planes = {}
    for ex in range(H + 1):
        y_planes[ex] = jnp.where(row + ex < bx, 1.0, beyond_x)

    def own_flags(e):
        kind, at, step = e
        k, mine = bond_of(step)
        if kind == "x":
            return intact[k, at].astype(jnp.float32) * B["scaled"][k] * beyond_x
        value = intact_flat[k, pl.ds(at, bx, stride=by), :].astype(jnp.float32) * B["lanes"][step[2] + H]
        return value * (y_planes[step[0]] * (terms(k)[0] * number(has["gy", 1 if step[1] > 0 else -1])))

    for e in x_list + y_list:
        if bond_of(e[2])[1]:
            B["hj"][place[e]] = own_flags(e)

    def length(d, k):
        long2 = d[0] * d[0] + d[1] * d[1] + d[2] * d[2]
        return long2, long2 * lax.rsqrt(long2) - radius_of(k)

    acc_t, acc_f = B["t", "sums"], B["u", "sums"]
    uz, tz = B["u", "main"], B["t", "main"]

    groups = [[k for k in ORDER if OFFSETS[k][0] == ex] for ex in range(H + 1)]

    def dilate(part, x, carry):
        mine = [u[c, x + H, own, :] for c in range(3)]
        near = [{v: mine[c] - float(v) if v else mine[c] for v in range(-H, H + 1)} for c in range(3)]
        total = zero
        for k in part:
            ex, ey, ez = OFFSETS[k]
            at = slice(PAD + ey, PAD + ey + by)
            d = [uz[ez + H, c, x + ex, at, :] - near[c][OFFSETS[k][c]] for c in range(3)]
            long2, ext = length(d, k)
            flags = intact[k, x].astype(jnp.float32) * B["scaled"][k]
            term = flags * ext
            B["jf"][k, x] = flags
            for c in range(3):
                B["d"][k, x, c] = d[c]
            B["ext"][k, x] = ext
            B["len"][k, x] = long2
            total = total + term
            acc_t[ez + H, x + ex, 0, at, :] += term
        B["t", "base"][0, x] = total if OFFSETS[part[0]][0] == 0 else B["t", "base"][0, x] + total
        return carry

    for ex, part in enumerate(groups):
        lax.fori_loop(0, bx - ex, functools.partial(dilate, part), 0)

    def gather(name):
        sums, base = B[name, "sums"], B[name, "base"]

        def body(x, carry):
            for c in range(base.shape[0]):
                value = base[c, x] + sums[H, x, c, own, :]
                for ez in (-2, -1, 1, 2, 3):
                    value = value + roll(sums[ez + H, x, c, own, :], ez) * B["lanes"][H - ez]
                base[c, x] = value
            return carry

        lax.fori_loop(0, bx, body, 0)

    gather("t")

    def soften_one(j, ext, long2, k):
        _, p, q = terms(k)
        more = (ext * ext) * (1.0 / (radius_of(k) * soft_stretch) ** 2 / p) + 1.0 / p
        return j * lax.rsqrt(more * more * long2), ext * (q / p)

    NEEDED = (0, 2, 2, 2, 2, 0)

    def beside_x(name):
        field, out = B[name, "field"], B[name, "x"]
        for c in range(field.shape[0]):
            for i in range(2 * H):
                value = field[c, i if i < H else i + bx, own, :]
                for ez in range(-NEEDED[i], NEEDED[i] + 1):
                    out[ez + H, c, i, own, :] = roll(value, -ez)

    def beside_y(name):
        field_flat, out = flat(B[name, "field"]), B[name, "y"]
        for c in range(out.shape[1]):
            for i in range(2 * H):
                at = PAD - H + i if i < H else PAD + by + i - H
                for half in range(2):
                    value = field_flat[c, pl.ds(half * bx * rows + at, bx, stride=rows), :]
                    for ez in range(-NEEDED[i], NEEDED[i] + 1):
                        out[ez + H, c, i, half * bx : half * bx + bx, :] = roll(value, -ez)

    def beside_z(name):
        z, out = B[name, "z"], B[name, "q"]
        for c in range(out.shape[1]):
            for tile in (slice(0, by), slice(by, rows)):
                near, left, right = [jnp.where(high, z[0, i, c, tile, :], z[1, i, c, tile, :]) for i in (1, 0, 2)]
                far = roll(jnp.where(lane < bz // 2 - GROUP, right, left), bx * GROUP)
                value = jnp.where(inner, near, far)
                for i, (ex, az) in enumerate(MOVES):
                    over = roll(value, GROUP - GROUP * ex - az)
                    under = roll(value, -GROUP - GROUP * ex + az)
                    out[i, c, tile, :] = jnp.where(high, over, under)

    def receive(sent, kind):
        for copy in sent:
            dx, dy, dz = copy.direction
            if ("z" if dz else "y" if dy else "x") == kind:
                copy.receive()

    strip_sign = jnp.where(high, 1.0, -1.0)

    def other(name, e, c):
        kind, at, (ex, ey, ez) = e
        if kind == "x":
            i = at + ex + H if at + ex < 0 else at + ex - bx + H
            return B[name, "x"][ez + H, c, i, PAD + ey : PAD + ey + by, :]
        if kind == "y":
            i = at + ey + H if at + ey < 0 else at + ey - by + H
            return B[name, "y"][ez + H, c, i, H + ex : H + ex + bx, :]
        return B[name, "q"][MOVES.index((ex, ez)), c, PAD + ey : PAD + ey + by, :]

    def inside(name, kind, at, c):
        if kind == "x":
            return B[name, "field"][c, at + H, own, :]
        if kind == "y":
            flat_field = u_flat if name == "u" else t_flat
            return flat_field[c, pl.ds(H * rows + PAD + at, bx, stride=rows), :]
        return B[name, "in"][c]

    def bond(e):
        return NUMBER[e[2]] if e[0] == "z" and e[2] in NUMBER else bond_of(e[2])[0]

    def add(name, kind, at, totals):
        base = B[name, "base"]
        for c, total in enumerate(totals):
            if kind == "x":
                base[c, at] += total
            else:
                base_flat = flat(base)
                base_flat[c, pl.ds(at, bx, stride=by), :] += total

    def stretch(part):
        near, was, total = {}, None, None
        for e in part:
            kind, at, step = e
            if (kind, at) != was:
                if was is not None:
                    add("t", *was, [total])
                was, near, total = (kind, at), {}, None
            i, k = place[e], bond(e)
            d = []
            for c in range(3):
                if (c, step[c]) not in near:
                    if (c, None) not in near:
                        near[c, None] = inside("u", kind, at, c)
                    start = near[c, None]
                    if step[c]:
                        move = strip_sign * float(step[c]) if kind == "z" and c == 2 else float(step[c])
                        start = start - move
                    near[c, step[c]] = start
                d.append(other("u", e, c) - near[c, step[c]])
            long2, ext = length(d, k)
            for c in range(3):
                B["hd"][i, c] = d[c]
            B["hext"][i] = ext
            B["hlen"][i] = long2
            term = B["hj"][i] * ext
            total = total + term if total is not None else term
        if was[0] == "z":
            return total
        add("t", *was, [total])

    def from_slots(ex, ey, az):
        got, s = B["slots"], SLOT[ex, ey, az]
        part = slice(PAD - ey, PAD - ey + by)
        value = jnp.where(high, got[0, 0, s, part, :], got[1, 0, s, part, :])
        if ex:
            far = jnp.where(high, got[0, 1, s, part, :], got[1, 1, s, part, :])
            value = jnp.where(inner, value, roll(far, bx * GROUP))
        over = roll(value, GROUP + GROUP * ex - az)
        under = roll(value, -GROUP + GROUP * ex + az)
        return jnp.where(spot >= GROUP - az, over, jnp.where(spot < az, under, 0.0))

    def taken_flags(e):
        kind, at, step = e
        ex, ey, ez = minus(step)
        k = NUMBER[ex, ey, ez]
        if kind == "x":
            value = B["ix"][k, at, PAD - ey : PAD - ey + by, :].astype(jnp.float32)
            return roll(value, ez) * (mask(*step[1:]) * terms(k)[0])
        from_row = at - ey + by if ey > 0 else at - ey - by
        value = iy_flat[k, pl.ds(from_row, bx, stride=by), :].astype(jnp.float32)
        return roll(value, ez) * (B["lanes"][step[2] + H] * terms(k)[0])

    own_x, taken_x = [[e for e in x_list if bond_of(e[2])[1] == mine] for mine in (True, False)]
    own_y, taken_y = [[e for e in y_list if bond_of(e[2])[1] == mine] for mine in (True, False)]
    receive(sent_u, "x")
    beside_x("u")
    stretch(own_x)
    receive(sent_u, "y")
    beside_y("u")
    stretch(own_y)
    receive(sent_u, "z")
    beside_z("u")
    receive(sent_i, "x")
    for e in taken_x:
        B["hj"][place[e]] = taken_flags(e)
    stretch(taken_x)
    receive(sent_i, "z")
    for e in z_list:
        ex, ey, az = e[2]
        value = B["own_slots"][SLOT[e[2]]] if e[2] in SLOT else None
        if (-ex, -ey, az) in SLOT:
            more = from_slots(-ex, -ey, az)
            value = more if value is None else value + more
        B["hj"][place[e]] = value
    strip_t = stretch(z_list)
    receive(sent_i, "y")
    for e in taken_y:
        B["hj"][place[e]] = taken_flags(e)
    stretch(taken_y)

    def finish(name, c, strip, write):
        base = B[name, "base"]
        for x, part in enumerate(unpack(strip)):
            write(x, base[c, x] + part)

    t = B["t", "field"]
    own_theta = []

    def write_theta(x, value):
        theta_out[x] = value
        t[0, x + H, own, :] = value
        own_theta.append(value)

    finish("t", 0, strip_t, write_theta)
    B["t", "in"][0] = pack(own_theta)
    sent_t = spread("t")

    shift_main("t")

    def push(part, x, carry):
        here = t[0, x + H, own, :]
        total = [zero, zero, zero]
        for k in part:
            ex, ey, ez = OFFSETS[k]
            at = slice(PAD + ey, PAD + ey + by)
            g, h = soften_one(B["jf"][k, x], B["ext"][k, x], B["len"][k, x], k)
            scalar = g * (here + tz[ez + H, 0, x + ex, at, :] + h)
            for c in range(3):
                pushed = scalar * B["d"][k, x, c]
                total[c] = total[c] + pushed
                acc_f[ez + H, x + ex, c, at, :] -= pushed
        for c in range(3):
            B["u", "base"][c, x] = total[c] if OFFSETS[part[0]][0] == 0 else B["u", "base"][c, x] + total[c]
        return carry

    for ex, part in enumerate(groups):
        lax.fori_loop(0, bx - ex, functools.partial(push, part), 0)
    gather("u")
    for e in everything:
        i = place[e]
        B["hlen"][i], B["hext"][i] = soften_one(B["hj"][i], B["hext"][i], B["hlen"][i], bond(e))

    for copy in copies:
        copy.finish()

    def forces(part):
        was, total = None, None
        for e in part:
            kind, at, _ = e
            if (kind, at) != was:
                if was is not None:
                    add("u", *was, total)
                was, total = (kind, at), None
                here = inside("t", kind, at, 0)
            i = place[e]
            scalar = B["hlen"][i] * (here + other("t", e, 0) + B["hext"][i])
            pushed = [scalar * B["hd"][i, c] for c in range(3)]
            total = [total[c] + pushed[c] for c in range(3)] if total is not None else pushed
        if was[0] == "z":
            return total
        add("u", *was, total)

    receive(sent_t, "x")
    beside_x("t")
    forces(x_list)
    receive(sent_t, "y")
    beside_y("t")
    forces(y_list)
    receive(sent_t, "z")
    beside_z("t")
    strip_f = forces(z_list)

    for c in range(3):

        def write_force(x, value, c=c):
            force_out[c, x] = value

        finish("u", c, strip_f[c], write_force)


def shards(sizes, displacement, bond_intact):
    plan = scratch_plan(bond_intact.shape[0], *displacement.shape[1:])
    scratch = [pltpu.VMEM(shape, dtype) for dtype, shape in plan.values()]
    scratch += [
        pltpu.VMEM(bond_intact.shape, jnp.int32),
        pltpu.SemaphoreType.DMA((96,)),
        pltpu.SemaphoreType.DMA((96,)),
        pltpu.SemaphoreType.DMA((2,)),
    ]
    vmem, anywhere = pl.BlockSpec(memory_space=pltpu.VMEM), pl.BlockSpec(memory_space=pl.ANY)
    return pl.pallas_call(
        functools.partial(kernel, sizes, tuple(plan)),
        out_shape=(
            jax.ShapeDtypeStruct(displacement.shape, jnp.float32),
            jax.ShapeDtypeStruct(displacement.shape[1:], jnp.float32),
        ),
        in_specs=[anywhere, anywhere],
        out_specs=(vmem, vmem),
        scratch_shapes=scratch,
        compiler_params=pltpu.CompilerParams(collective_id=0, has_side_effects=True, vmem_limit_bytes=56375000),
    )(displacement, bond_intact)


def solution(mesh):
    sizes = {a: mesh.shape[a] for a in AXES}
    return jax.shard_map(
        functools.partial(shards, sizes),
        mesh=mesh,
        in_specs=(P(None, "gx", "gy", "gz"), P(None, "gx", "gy", "gz")),
        out_specs=(P(None, "gx", "gy", "gz"), P("gx", "gy", "gz")),
        check_vma=False,
    )
```

```python
import functools
import math

import jax
import jax.numpy as jnp
from jax import lax
from jax.experimental import pallas as pl
from jax.experimental.pallas import tpu as pltpu
from jax.sharding import PartitionSpec as P

MESH = pl.DeviceIdType.MESH
bulk_modulus = 150.0
shear_modulus = 25.0
soft_stretch = 0.05
AXES = ("gx", "gy", "gz")
H = 3
PAD = 4
GROUP = 8


def bond_offsets():
    chosen = []
    for step_x in range(0, 4):
        for step_y in range(-3, 4):
            for step_z in range(-3, 4):
                if step_x * step_x + step_y * step_y + step_z * step_z > 9:
                    continue
                if step_x > 0 or (step_x == 0 and (step_y > 0 or (step_y == 0 and step_z > 0))):
                    chosen.append((step_x, step_y, step_z))
    return chosen


OFFSETS = bond_offsets()
NUMBER = {o: k for k, o in enumerate(OFFSETS)}
ORDER = sorted(range(len(OFFSETS)), key=lambda k: (OFFSETS[k][:2], OFFSETS[k][2]))


def square(offset):
    return sum(step * step for step in offset)


VOLUME = 2.0 * sum(math.exp(-square(o) / 9.0) * square(o) for o in OFFSETS)


def minus(offset):
    return tuple(-step for step in offset)


def bond_of(step):
    return (NUMBER[step], True) if step in NUMBER else (NUMBER[minus(step)], False)


def radius_of(k):
    return math.sqrt(square(OFFSETS[k]))


def terms(k):
    weight, radius = math.exp(-square(OFFSETS[k]) / 9.0), radius_of(k)
    c = 3.0 / VOLUME * weight * radius
    a = 3.0 * bulk_modulus / VOLUME * weight * radius
    b = 15.0 * shear_modulus / VOLUME * weight
    return c, (a - b * radius / 3.0) / c, 2.0 * b / c


STEPS = [s for o in OFFSETS for s in (o, minus(o))]
PAIRS = sorted({s[1:] for s in STEPS})
FIRST = {}
LAST = {}
for _k, _o in enumerate(OFFSETS):
    FIRST.setdefault(_o[0], _k)
    LAST[_o[0]] = _k + 1
RUNS = {}
for _k, _o in enumerate(OFFSETS):
    if _o[1]:
        RUNS.setdefault(_o[:2], []).append(_k)
RUNS = {g: (ks[0], ks[-1] + 1) for g, ks in RUNS.items()}

SLOTS = sorted(
    {(o[0], o[1], abs(o[2])) for o in OFFSETS if o[2]},
    key=lambda s: ((0 if s[1] > 0 else 1 if s[1] < 0 else 2), s[0] if s[1] else -s[0], s),
)
SLOT = {s: i for i, s in enumerate(SLOTS)}
STRIP = sorted({(s[0], s[1], abs(s[2])) for s in STEPS if s[2]})
MOVES = sorted({(s[0], s[2]) for s in STRIP})


TILES = []
WHERE = {}
for _s in SLOTS:
    _kind = (_s[1] > 0, _s[1] < 0, _s[0] > 0)
    if TILES and len(TILES[-1][1]) == 1 and TILES[-1][0] == _kind:
        WHERE[_s] = (len(TILES) - 1, True)
        TILES[-1][1].append(_s)
    else:
        WHERE[_s] = (len(TILES), False)
        TILES.append((_kind, [_s]))


def span(test):
    found = [i for i, (_, pair) in enumerate(TILES) if test(pair[0])]
    assert found == list(range(found[0], found[-1] + 1))
    return slice(found[0], found[-1] + 1)


def side(step, size, at):
    return slice(at - H, at) if step < 0 else slice(at + size, at + size + H) if step > 0 else slice(at, at + size)


def edge_of(step, size, at):
    return slice(at, at + H) if step < 0 else slice(at + size - H, at + size) if step > 0 else slice(at, at + size)


def evaluations(bx, by):
    x_list, y_list = [], []
    for x in range(bx):
        x_list += [("x", x, s) for s in sorted(STEPS, key=lambda s: (s[1], s[2])) if not 0 <= x + s[0] < bx]
    for r in range(by):
        y_list += [("y", r, s) for s in sorted(STEPS, key=lambda s: (s[0], s[2])) if not 0 <= r + s[1] < by]
    return x_list, y_list, [("z", 0, s) for s in STRIP]


def scratch_plan(bonds, bx, by, bz):
    rows, planes, f, i = by + 2 * PAD, 2 * bx, jnp.float32, jnp.int32
    halo = sum(len(part) for part in evaluations(bx, by))
    plan = {"jf": (f, (bonds, bx, by, bz)), "ext": (f, (bonds, bx, by, bz)), "len": (f, (bonds, bx, by, bz))}
    plan["d"] = (f, (bonds, bx, 3, by, bz))
    plan["hj"] = plan["hext"] = plan["hlen"] = (f, (halo, by, bz))
    plan["hd"] = (f, (halo, 3, by, bz))
    plan["mask"] = (f, (len(PAIRS), by, bz))
    plan["lanes"] = (f, (7, by, bz))
    plan["scaled"] = (f, (bonds, by, bz))
    plan["ix"] = (i, (bonds, H, rows, bz))
    plan["iy"] = (i, (bonds, bx, by, bz))
    plan["own_slots"] = (f, (len(SLOTS), by, bz))
    plan["slots"] = (f, (2, 2, len(TILES), rows, bz))
    plan["sent_slots"] = (f, (2, len(TILES), by, bz))
    for name, c in (("u", 3), ("t", 1)):
        plan[name, "field"] = (f, (c, planes, rows, bz))
        plan[name, "main"] = (f, (7, c, bx, rows, bz))
        plan[name, "sums"] = (f, (7, bx, c, rows, bz))
        plan[name, "base"] = (f, (c, bx, by, bz))
        plan[name, "x"] = (f, (7, c, 2 * H, rows, bz))
        plan[name, "y"] = (f, (7, c, 2 * H, planes, bz))
        plan[name, "in"] = (f, (c, by, bz))
        plan[name, "z"] = (f, (2, 3, c, rows, bz))
        plan[name, "q"] = (f, (len(MOVES), c, rows, bz))
    return plan


def kernel(sizes, names, u_hbm, intact_hbm, force_out, theta_out, *scratch):
    B = dict(zip(names, scratch))
    intact, send_sem, recv_sem, load_sem = scratch[len(names) :]
    bx, by, bz = theta_out.shape
    rows, planes = by + 2 * PAD, 2 * bx
    assert bx == by and planes * GROUP == bz and GROUP >= 2 * H + 2
    x_list, y_list, z_list = evaluations(bx, by)
    everything = x_list + y_list + z_list
    place = {e: i for i, e in enumerate(everything)}
    index = {a: lax.axis_index(a) for a in AXES}
    has = {(a, -1): index[a] > 0 for a in AXES}
    has.update({(a, 1): index[a] < sizes[a] - 1 for a in AXES})
    own = slice(PAD, PAD + by)

    def there(direction):
        found = None
        for a, step in zip(AXES, direction):
            if step:
                found = has[a, step] if found is None else found & has[a, step]
        return found

    everyone = [(x, y, z) for x in (-1, 0, 1) for y in (-1, 0, 1) for z in (-1, 0, 1) if x or y or z]
    exists = {d: there(d) for d in everyone}

    def device(direction):
        return {a: index[a] + step for a, step in zip(AXES, direction) if step}

    u = B["u", "field"]
    load_u = pltpu.make_async_copy(u_hbm, u.at[:, H : H + bx, own, :], load_sem.at[0])
    load_u.start()
    load = pltpu.make_async_copy(intact_hbm, intact, load_sem.at[1])
    load.start()

    barrier = pltpu.get_barrier_semaphore()
    count = jnp.int32(0)
    for d in sorted(everyone, key=lambda d: -sum(map(abs, d))):
        count = count + jnp.where(exists[d], 1, 0).astype(jnp.int32)

        @pl.when(exists[d])
        def _(d=d):
            pl.semaphore_signal(barrier, inc=1, device_id=device(d), device_id_type=MESH)

    copies = []

    class Shift:
        def __init__(self, direction, src, dst):
            number = len(copies)
            copies.append(self)
            self.direction = direction
            self.copy = pltpu.make_async_remote_copy(
                src_ref=src, dst_ref=dst, send_sem=send_sem.at[number], recv_sem=recv_sem.at[number],
                device_id=device(direction), device_id_type=MESH,
            )
            self.sends = exists[direction]
            self.takes = exists[minus(direction)]

            @pl.when(self.sends)
            def _():
                self.copy.start()

        def receive(self):
            @pl.when(self.takes)
            def _():
                self.copy.wait_recv()

        def finish(self):
            @pl.when(self.sends)
            def _():
                self.copy.wait_send()

    def nothing(view):
        view[...] = jnp.zeros(view.shape, view.dtype)

    def landing(name, d):
        if d[2]:
            return B[name, "z"].at[(d[2] + 1) // 2, d[0] + 1, :, side(d[1], by, PAD), :]
        return B[name, "field"].at[:, side(d[0], bx, H), side(d[1], by, PAD), :]

    SENT = (slice(0, by), slice(by - 2, by), slice(0, 2))
    LAND = (slice(PAD, PAD + by), slice(PAD - 2, PAD), slice(PAD + by, PAD + by + 2))
    up, down = span(lambda s: s[1] > 0), span(lambda s: s[1] < 0)
    x_all, x_up = span(lambda s: s[0] > 0), span(lambda s: s[0] > 0 and s[1] > 0)
    slot_moves = []
    for dz in (-1, 1):
        for dx, parts in ((0, (slice(0, len(TILES)), up, down)), (1, (x_all, x_up, down))):
            for way, dy in enumerate((0, 1, -1)):
                slot_moves.append(((dx, dy, dz), parts[way], way))

    def slot_landing(d, part, way):
        return B["slots"].at[(1 - d[2]) // 2, d[0], part, LAND[way], :]

    lane = lax.broadcasted_iota(jnp.int32, (by, bz), 1)
    row = lax.broadcasted_iota(jnp.int32, (by, bz), 0)
    spot = lax.rem(lane, GROUP)
    high = spot >= GROUP // 2
    edge = (lane < H) | (lane >= bz - H)
    inner = (lane >= H * GROUP) & (lane < (H + bx) * GROUP)
    zero = jnp.zeros((by, bz), jnp.float32)

    def number(condition):
        return jnp.where(condition, 1.0, 0.0)

    def roll(value, amount):
        return pltpu.roll(value, amount % bz, 1) if amount % bz else value

    def to_strip(total):
        return jnp.where(high, roll(total, GROUP), total)

    def pack(tiles):
        total = zero
        for x, tile in enumerate(tiles):
            total = total + roll(jnp.where(edge, tile, 0.0), GROUP * (x + H))
        return to_strip(total)

    def unpack(strip):
        strip = jnp.where(high, roll(strip, -GROUP), strip)
        return [jnp.where(edge, roll(strip, -GROUP * (x + H)), 0.0) for x in range(bx)]

    def flat(ref, *at):
        return ref.reshape(*ref.shape[:-3], ref.shape[-3] * ref.shape[-2], bz)

    u_flat, t_flat, intact_flat = flat(u), flat(B["t", "field"]), flat(intact)
    iy_flat = flat(B["iy"])

    def clear(ref, depth):
        zeros = jnp.zeros(ref.shape[2:], jnp.float32)

        def body(i, carry):
            for s in range(1, depth):
                ref[s, i] = zeros
            return carry

        lax.fori_loop(0, ref.shape[1], body, 0)

    def mask(ey, ez):
        return B["mask"][PAIRS.index((ey, ez))]

    def shift_main(name):
        field, out = B[name, "field"], B[name, "main"]

        def body(x, carry):
            for c in range(field.shape[0]):
                value = field[c, x + H, own, :]
                for ez in range(1 - H, H + 1):
                    moved = roll(value, -ez)
                    out[ez + H, c, x, own, :] = moved
                    out[ez + H, c, x, 0:PAD, :] = moved[0:PAD]
                    out[ez + H, c, x, PAD + by :, :] = moved[0:PAD]
            return carry

        lax.fori_loop(0, bx, body, 0)

    load_u.wait()
    for c in range(3):
        B["u", "in"][c] = pack([u[c, x + H, own, :] for x in range(bx)])
    load.wait()

    beyond_x = number(has["gx", 1])
    z_up, z_down = number(has["gz", 1]), number(has["gz", -1])

    def slots_body(x, totals):
        new = []
        crossing = jnp.where(has["gx", 1], 1.0, 0.0)
        for (ex, ey, az), total in zip(SLOTS, totals):
            value = jnp.where(lane >= bz - az, intact[NUMBER[ex, ey, az], x].astype(jnp.float32) * z_up, 0.0)
            if (ex, ey, -az) in NUMBER:
                other = intact[NUMBER[ex, ey, -az], x].astype(jnp.float32) * z_down
                value = jnp.where(lane < az, other, value)
            if ex:
                value = value * jnp.where(x + ex < bx, 1.0, crossing)
            new.append(total + pltpu.roll(value, GROUP * (x + H), 1))
        return tuple(new)

    totals = lax.fori_loop(0, bx, slots_body, tuple(zero for _ in SLOTS))
    y_inside = {}
    for ey in range(-H, H + 1):
        inside = (row + ey >= 0) & (row + ey < by)
        y_inside[ey] = jnp.where(inside, 1.0, number(has["gy", 1 if ey > 0 else -1])) if ey else None
    for (ex, ey, az), total in zip(SLOTS, totals):
        value = to_strip(total) * terms(NUMBER[ex, ey, az])[0]
        B["own_slots"][SLOT[ex, ey, az]] = value * y_inside[ey] if ey else value
    for i, (_, pair) in enumerate(TILES):
        one = B["own_slots"][SLOT[pair[0]]]
        for way, move in ((0, GROUP // 2), (1, -GROUP // 2)):
            value = one
            if len(pair) == 2:
                two = roll(B["own_slots"][SLOT[pair[1]]], move)
                value = jnp.where(high, one, two) if way else jnp.where(high, two, one)
            B["sent_slots"][way, i] = value

    pl.semaphore_wait(barrier, count)

    def spread(name):
        field, strip = B[name, "field"], B[name, "in"]
        sent = []
        for d in sorted(everyone, key=lambda d: -sum(map(abs, d))):
            if d[2]:
                src = strip.at[:, edge_of(d[1], by, 0), :]
            else:
                src = field.at[:, edge_of(d[0], bx, H), edge_of(d[1], by, PAD), :]
            sent.append(Shift(d, src, landing(name, minus(d))))
        return sent

    sent_u = spread("u")
    sent_i = []
    ends = {g: (slice(by - g[1], by) if g[1] > 0 else slice(0, -g[1])) for g in RUNS}
    for (ex, ey), (k0, k1) in RUNS.items():
        src = intact.at[k0:k1, 0 : bx - ex, ends[ex, ey], :]
        sent_i.append(Shift((0, 1 if ey > 0 else -1, 0), src, B["iy"].at[k0:k1, ex:, ends[ex, ey], :]))
    for e, part, way in reversed(slot_moves):
        sent_i.append(Shift(e, B["sent_slots"].at[(e[2] + 1) // 2, part, SENT[way], :], slot_landing(e, part, way)))
    for (ex, ey), (k0, k1) in RUNS.items():
        if ex:
            src = intact.at[k0:k1, bx - ex :, ends[ex, ey], :]
            sent_i.append(Shift((1, 1 if ey > 0 else -1, 0), src, B["iy"].at[k0:k1, 0:ex, ends[ex, ey], :]))
    for ex in range(1, H + 1):
        k0, k1 = FIRST[ex], LAST[ex]
        sent_i.append(Shift((1, 0, 0), intact.at[k0:k1, bx - ex :, :, :], B["ix"].at[k0:k1, 0:ex, own, :]))


    for d in everyone:

        @pl.when(jnp.logical_not(exists[d]))
        def _(d=d):
            for name in ("u", "t"):
                nothing(landing(name, d))
            for e, part, way in slot_moves:
                if minus(e) == d:
                    nothing(slot_landing(e, part, way))
            if d == (-1, 0, 0):
                for ex in range(1, H + 1):
                    nothing(B["ix"].at[FIRST[ex] : LAST[ex], 0:ex, own, :])
            for (ex, ey), (k0, k1) in RUNS.items():
                back = -1 if ey > 0 else 1
                at = slice(by - ey, by) if ey > 0 else slice(0, -ey)
                if d == (0, back, 0):
                    nothing(B["iy"].at[k0:k1, ex:, at, :])
                if ex and d == (-1, back, 0):
                    nothing(B["iy"].at[k0:k1, 0:ex, at, :])


    for i, (ey, ez) in enumerate(PAIRS):
        B["mask"][i] = number((row + ey >= 0) & (row + ey < by) & (lane + ez >= 0) & (lane + ez < bz))
    for ez in range(-H, H + 1):
        B["lanes"][ez + H] = number((lane + ez >= 0) & (lane + ez < bz))

    def blank_rows(i, carry):
        for name in ("u", "t"):
            out = B[name, "x"]
            for c in range(out.shape[1]):
                for s in range(7):
                    for part in (slice(0, PAD), slice(PAD + by, rows)):
                        out[s, c, i, part, :] = jnp.zeros((PAD, bz), jnp.float32)
        return carry

    lax.fori_loop(0, 2 * H, blank_rows, 0)

    clear(B["t", "sums"], 7)
    clear(B["u", "sums"], 7)
    for k, (ex, ey, ez) in enumerate(OFFSETS):
        B["scaled"][k] = mask(ey, ez) * terms(k)[0]

    shift_main("u")

    y_planes = {}
    for ex in range(H + 1):
        y_planes[ex] = jnp.where(row + ex < bx, 1.0, beyond_x)

    def own_flags(e):
        kind, at, step = e
        k, mine = bond_of(step)
        if kind == "x":
            return intact[k, at].astype(jnp.float32) * B["scaled"][k] * beyond_x
        value = intact_flat[k, pl.ds(at, bx, stride=by), :].astype(jnp.float32) * B["lanes"][step[2] + H]
        return value * (y_planes[step[0]] * (terms(k)[0] * number(has["gy", 1 if step[1] > 0 else -1])))

    for e in x_list + y_list:
        if bond_of(e[2])[1]:
            B["hj"][place[e]] = own_flags(e)

    def length(d, k):
        long2 = d[0] * d[0] + d[1] * d[1] + d[2] * d[2]
        return long2, long2 * lax.rsqrt(long2) - radius_of(k)

    acc_t, acc_f = B["t", "sums"], B["u", "sums"]
    uz, tz = B["u", "main"], B["t", "main"]

    groups = [[k for k in ORDER if OFFSETS[k][0] == ex] for ex in range(H + 1)]

    def dilate(part, x, carry):
        mine = [u[c, x + H, own, :] for c in range(3)]
        near = [{v: mine[c] - float(v) if v else mine[c] for v in range(-H, H + 1)} for c in range(3)]
        total = zero
        for k in part:
            ex, ey, ez = OFFSETS[k]
            at = slice(PAD + ey, PAD + ey + by)
            d = [uz[ez + H, c, x + ex, at, :] - near[c][OFFSETS[k][c]] for c in range(3)]
            long2, ext = length(d, k)
            flags = intact[k, x].astype(jnp.float32) * B["scaled"][k]
            term = flags * ext
            B["jf"][k, x] = flags
            for c in range(3):
                B["d"][k, x, c] = d[c]
            B["ext"][k, x] = ext
            B["len"][k, x] = long2
            total = total + term
            acc_t[ez + H, x + ex, 0, at, :] += term
        B["t", "base"][0, x] = total if OFFSETS[part[0]][0] == 0 else B["t", "base"][0, x] + total
        return carry

    for ex, part in enumerate(groups):
        lax.fori_loop(0, bx - ex, functools.partial(dilate, part), 0)

    def gather(name):
        sums, base = B[name, "sums"], B[name, "base"]

        def body(x, carry):
            for c in range(base.shape[0]):
                value = base[c, x] + sums[H, x, c, own, :]
                for ez in (-2, -1, 1, 2, 3):
                    value = value + roll(sums[ez + H, x, c, own, :], ez) * B["lanes"][H - ez]
                base[c, x] = value
            return carry

        lax.fori_loop(0, bx, body, 0)

    gather("t")

    def soften_one(j, ext, long2, k):
        _, p, q = terms(k)
        more = (ext * ext) * (1.0 / (radius_of(k) * soft_stretch) ** 2 / p) + 1.0 / p
        return j * lax.rsqrt(more * more * long2), ext * (q / p)

    NEEDED = (0, 2, 2, 2, 2, 0)

    def beside_x(name):
        field, out = B[name, "field"], B[name, "x"]
        for c in range(field.shape[0]):
            for i in range(2 * H):
                value = field[c, i if i < H else i + bx, own, :]
                for ez in range(-NEEDED[i], NEEDED[i] + 1):
                    out[ez + H, c, i, own, :] = roll(value, -ez)

    def beside_y(name):
        field_flat, out = flat(B[name, "field"]), B[name, "y"]
        for c in range(out.shape[1]):
            for i in range(2 * H):
                at = PAD - H + i if i < H else PAD + by + i - H
                for half in range(2):
                    value = field_flat[c, pl.ds(half * bx * rows + at, bx, stride=rows), :]
                    for ez in range(-NEEDED[i], NEEDED[i] + 1):
                        out[ez + H, c, i, half * bx : half * bx + bx, :] = roll(value, -ez)

    def beside_z(name):
        z, out = B[name, "z"], B[name, "q"]
        for c in range(out.shape[1]):
            for tile in (slice(0, by), slice(by, rows)):
                near, left, right = [jnp.where(high, z[0, i, c, tile, :], z[1, i, c, tile, :]) for i in (1, 0, 2)]
                far = roll(jnp.where(lane < bz // 2 - GROUP, right, left), bx * GROUP)
                value = jnp.where(inner, near, far)
                for i, (ex, az) in enumerate(MOVES):
                    over = roll(value, GROUP - GROUP * ex - az)
                    under = roll(value, -GROUP - GROUP * ex + az)
                    out[i, c, tile, :] = jnp.where(high, over, under)

    def receive(sent, kind):
        for copy in sent:
            dx, dy, dz = copy.direction
            if ("z" if dz else "y" if dy else "x") == kind:
                copy.receive()

    strip_sign = jnp.where(high, 1.0, -1.0)

    def other(name, e, c):
        kind, at, (ex, ey, ez) = e
        if kind == "x":
            i = at + ex + H if at + ex < 0 else at + ex - bx + H
            return B[name, "x"][ez + H, c, i, PAD + ey : PAD + ey + by, :]
        if kind == "y":
            i = at + ey + H if at + ey < 0 else at + ey - by + H
            return B[name, "y"][ez + H, c, i, H + ex : H + ex + bx, :]
        return B[name, "q"][MOVES.index((ex, ez)), c, PAD + ey : PAD + ey + by, :]

    def inside(name, kind, at, c):
        if kind == "x":
            return B[name, "field"][c, at + H, own, :]
        if kind == "y":
            flat_field = u_flat if name == "u" else t_flat
            return flat_field[c, pl.ds(H * rows + PAD + at, bx, stride=rows), :]
        return B[name, "in"][c]

    def bond(e):
        return NUMBER[e[2]] if e[0] == "z" and e[2] in NUMBER else bond_of(e[2])[0]

    def add(name, kind, at, totals):
        base = B[name, "base"]
        for c, total in enumerate(totals):
            if kind == "x":
                base[c, at] += total
            else:
                base_flat = flat(base)
                base_flat[c, pl.ds(at, bx, stride=by), :] += total

    def stretch(part, flags_known):
        near, was, total = {}, None, None
        for e in part:
            kind, at, step = e
            if (kind, at) != was:
                if was is not None and flags_known:
                    add("t", *was, [total])
                was, near, total = (kind, at), {}, None
            i, k = place[e], bond(e)
            d = []
            for c in range(3):
                if (c, step[c]) not in near:
                    if (c, None) not in near:
                        near[c, None] = inside("u", kind, at, c)
                    start = near[c, None]
                    if step[c]:
                        move = strip_sign * float(step[c]) if kind == "z" and c == 2 else float(step[c])
                        start = start - move
                    near[c, step[c]] = start
                d.append(other("u", e, c) - near[c, step[c]])
            long2, ext = length(d, k)
            for c in range(3):
                B["hd"][i, c] = d[c]
            B["hext"][i] = ext
            B["hlen"][i] = long2
            if flags_known:
                term = B["hj"][i] * ext
                total = total + term if total is not None else term
        if flags_known:
            add("t", *was, [total])

    def weigh(part, flags_of):
        was, total = None, None
        for e in part:
            if e[:2] != was:
                if was is not None:
                    add("t", *was, [total])
                was, total = e[:2], None
            flags = flags_of(e)
            B["hj"][place[e]] = flags
            term = flags * B["hext"][place[e]]
            total = total + term if total is not None else term
        if was[0] == "z":
            return total
        add("t", *was, [total])

    def from_slots(ex, ey, az):
        got, (s, second) = B["slots"], WHERE[ex, ey, az]
        part = slice(PAD - ey, PAD - ey + by)
        a, b, move = (1, 0, GROUP // 2) if second else (0, 1, 0)
        value = jnp.where(high, got[a, 0, s, part, :], got[b, 0, s, part, :])
        if ex:
            far = jnp.where(high, got[a, 1, s, part, :], got[b, 1, s, part, :])
            value = jnp.where(inner, value, roll(far, bx * GROUP))
        over = roll(value, GROUP + GROUP * ex - az - move)
        under = roll(value, -GROUP + GROUP * ex + az + move)
        return jnp.where(spot >= GROUP - az, over, jnp.where(spot < az, under, 0.0))

    def taken_flags(e):
        kind, at, step = e
        ex, ey, ez = minus(step)
        k = NUMBER[ex, ey, ez]
        if kind == "x":
            value = B["ix"][k, at, PAD - ey : PAD - ey + by, :].astype(jnp.float32)
            return roll(value, ez) * (mask(*step[1:]) * terms(k)[0])
        from_row = at - ey + by if ey > 0 else at - ey - by
        value = iy_flat[k, pl.ds(from_row, bx, stride=by), :].astype(jnp.float32)
        return roll(value, ez) * (B["lanes"][step[2] + H] * terms(k)[0])

    own_x, taken_x = [[e for e in x_list if bond_of(e[2])[1] == mine] for mine in (True, False)]
    own_y, taken_y = [[e for e in y_list if bond_of(e[2])[1] == mine] for mine in (True, False)]

    def strip_flags(e):
        ex, ey, az = e[2]
        value = B["own_slots"][SLOT[e[2]]] if e[2] in SLOT else None
        if (-ex, -ey, az) in SLOT:
            more = from_slots(-ex, -ey, az)
            value = more if value is None else value + more
        return value

    receive(sent_u, "x")
    beside_x("u")
    stretch(own_x, True)
    stretch(taken_x, False)
    receive(sent_u, "y")
    beside_y("u")
    stretch(own_y, True)
    stretch(taken_y, False)
    receive(sent_u, "z")
    beside_z("u")
    stretch(z_list, False)
    receive(sent_i, "x")
    weigh(taken_x, taken_flags)
    receive(sent_i, "z")
    strip_t = weigh(z_list, strip_flags)
    receive(sent_i, "y")
    weigh(taken_y, taken_flags)

    def finish(name, c, strip, write):
        base = B[name, "base"]
        for x, part in enumerate(unpack(strip)):
            write(x, base[c, x] + part)

    t = B["t", "field"]

    def write_theta(x, value):
        theta_out[x] = value
        t[0, x + H, own, :] = value

    B["t", "in"][0] = pack([B["t", "base"][0, x] for x in range(bx)]) + strip_t
    finish("t", 0, strip_t, write_theta)
    sent_t = spread("t")

    shift_main("t")

    def push(part, x, carry):
        here = t[0, x + H, own, :]
        total = [zero, zero, zero]
        for k in part:
            ex, ey, ez = OFFSETS[k]
            at = slice(PAD + ey, PAD + ey + by)
            g, h = soften_one(B["jf"][k, x], B["ext"][k, x], B["len"][k, x], k)
            scalar = g * (here + tz[ez + H, 0, x + ex, at, :] + h)
            for c in range(3):
                pushed = scalar * B["d"][k, x, c]
                total[c] = total[c] + pushed
                acc_f[ez + H, x + ex, c, at, :] -= pushed
        for c in range(3):
            B["u", "base"][c, x] = total[c] if OFFSETS[part[0]][0] == 0 else B["u", "base"][c, x] + total[c]
        return carry

    for ex, part in enumerate(groups):
        lax.fori_loop(0, bx - ex, functools.partial(push, part), 0)
    gather("u")
    for e in everything:
        i = place[e]
        B["hlen"][i], B["hext"][i] = soften_one(B["hj"][i], B["hext"][i], B["hlen"][i], bond(e))

    for copy in copies:
        copy.finish()

    def forces(part):
        was, total = None, None
        for e in part:
            kind, at, _ = e
            if (kind, at) != was:
                if was is not None:
                    add("u", *was, total)
                was, total = (kind, at), None
                here = inside("t", kind, at, 0)
            i = place[e]
            scalar = B["hlen"][i] * (here + other("t", e, 0) + B["hext"][i])
            pushed = [scalar * B["hd"][i, c] for c in range(3)]
            total = [total[c] + pushed[c] for c in range(3)] if total is not None else pushed
        if was[0] == "z":
            return total
        add("u", *was, total)

    receive(sent_t, "x")
    beside_x("t")
    forces(x_list)
    receive(sent_t, "y")
    beside_y("t")
    forces(y_list)
    receive(sent_t, "z")
    beside_z("t")
    strip_f = forces(z_list)

    for c in range(3):

        def write_force(x, value, c=c):
            force_out[c, x] = value

        finish("u", c, strip_f[c], write_force)


def shards(sizes, displacement, bond_intact):
    plan = scratch_plan(bond_intact.shape[0], *displacement.shape[1:])
    scratch = [pltpu.VMEM(shape, dtype) for dtype, shape in plan.values()]
    scratch += [
        pltpu.VMEM(bond_intact.shape, jnp.int32),
        pltpu.SemaphoreType.DMA((96,)),
        pltpu.SemaphoreType.DMA((96,)),
        pltpu.SemaphoreType.DMA((2,)),
    ]
    vmem, anywhere = pl.BlockSpec(memory_space=pltpu.VMEM), pl.BlockSpec(memory_space=pl.ANY)
    return pl.pallas_call(
        functools.partial(kernel, sizes, tuple(plan)),
        out_shape=(
            jax.ShapeDtypeStruct(displacement.shape, jnp.float32),
            jax.ShapeDtypeStruct(displacement.shape[1:], jnp.float32),
        ),
        in_specs=[anywhere, anywhere],
        out_specs=(vmem, vmem),
        scratch_shapes=scratch,
        compiler_params=pltpu.CompilerParams(collective_id=0, has_side_effects=True, vmem_limit_bytes=56375000),
    )(displacement, bond_intact)


def solution(mesh):
    sizes = {a: mesh.shape[a] for a in AXES}
    return jax.shard_map(
        functools.partial(shards, sizes),
        mesh=mesh,
        in_specs=(P(None, "gx", "gy", "gz"), P(None, "gx", "gy", "gz")),
        out_specs=(P(None, "gx", "gy", "gz"), P("gx", "gy", "gz")),
        check_vma=False,
    )
```

```python
import functools
import math

import jax
import jax.numpy as jnp
from jax import lax
from jax.experimental import pallas as pl
from jax.experimental.pallas import tpu as pltpu
from jax.sharding import PartitionSpec as P

MESH = pl.DeviceIdType.MESH
bulk_modulus = 150.0
shear_modulus = 25.0
soft_stretch = 0.05
AXES = ("gx", "gy", "gz")
H = 3
PAD = 4
GROUP = 8


def bond_offsets():
    chosen = []
    for step_x in range(0, 4):
        for step_y in range(-3, 4):
            for step_z in range(-3, 4):
                if step_x * step_x + step_y * step_y + step_z * step_z > 9:
                    continue
                if step_x > 0 or (step_x == 0 and (step_y > 0 or (step_y == 0 and step_z > 0))):
                    chosen.append((step_x, step_y, step_z))
    return chosen


OFFSETS = bond_offsets()
NUMBER = {o: k for k, o in enumerate(OFFSETS)}
ORDER = sorted(range(len(OFFSETS)), key=lambda k: (OFFSETS[k][:2], OFFSETS[k][2]))


def square(offset):
    return sum(step * step for step in offset)


VOLUME = 2.0 * sum(math.exp(-square(o) / 9.0) * square(o) for o in OFFSETS)


def minus(offset):
    return tuple(-step for step in offset)


def bond_of(step):
    return (NUMBER[step], True) if step in NUMBER else (NUMBER[minus(step)], False)


def radius_of(k):
    return math.sqrt(square(OFFSETS[k]))


def terms(k):
    weight, radius = math.exp(-square(OFFSETS[k]) / 9.0), radius_of(k)
    c = 3.0 / VOLUME * weight * radius
    a = 3.0 * bulk_modulus / VOLUME * weight * radius
    b = 15.0 * shear_modulus / VOLUME * weight
    return c, (a - b * radius / 3.0) / c, 2.0 * b / c


STEPS = [s for o in OFFSETS for s in (o, minus(o))]
PAIRS = sorted({s[1:] for s in STEPS})
FIRST = {}
LAST = {}
for _k, _o in enumerate(OFFSETS):
    FIRST.setdefault(_o[0], _k)
    LAST[_o[0]] = _k + 1
RUNS = {}
for _k, _o in enumerate(OFFSETS):
    if _o[1]:
        RUNS.setdefault(_o[:2], []).append(_k)
RUNS = {g: (ks[0], ks[-1] + 1) for g, ks in RUNS.items()}

SLOTS = sorted(
    {(o[0], o[1], abs(o[2])) for o in OFFSETS if o[2]},
    key=lambda s: ((0 if s[1] > 0 else 1 if s[1] < 0 else 2), s[0] if s[1] else -s[0], s),
)
SLOT = {s: i for i, s in enumerate(SLOTS)}
STRIP = sorted({(s[0], s[1], abs(s[2])) for s in STEPS if s[2]})
MOVES = sorted({(s[0], s[2]) for s in STRIP})


TILES = []
WHERE = {}
for _s in SLOTS:
    _kind = (_s[1] > 0, _s[1] < 0, _s[0] > 0)
    if TILES and len(TILES[-1][1]) == 1 and TILES[-1][0] == _kind:
        WHERE[_s] = (len(TILES) - 1, True)
        TILES[-1][1].append(_s)
    else:
        WHERE[_s] = (len(TILES), False)
        TILES.append((_kind, [_s]))


def span(test):
    found = [i for i, (_, pair) in enumerate(TILES) if test(pair[0])]
    assert found == list(range(found[0], found[-1] + 1))
    return slice(found[0], found[-1] + 1)


def side(step, size, at):
    return slice(at - H, at) if step < 0 else slice(at + size, at + size + H) if step > 0 else slice(at, at + size)


def edge_of(step, size, at):
    return slice(at, at + H) if step < 0 else slice(at + size - H, at + size) if step > 0 else slice(at, at + size)


def evaluations(bx, by):
    x_list, y_list = [], []
    for x in range(bx):
        x_list += [("x", x, s) for s in sorted(STEPS, key=lambda s: (s[1], s[2])) if not 0 <= x + s[0] < bx]
    for r in range(by):
        y_list += [("y", r, s) for s in sorted(STEPS, key=lambda s: (s[0], s[2])) if not 0 <= r + s[1] < by]
    return x_list, y_list, [("z", 0, s) for s in STRIP]


def scratch_plan(bonds, bx, by, bz):
    rows, planes, f, i = by + 2 * PAD, 2 * bx, jnp.float32, jnp.int32
    halo = sum(len(part) for part in evaluations(bx, by))
    plan = {"jf": (f, (bonds, bx, by, bz)), "ext": (f, (bonds, bx, by, bz)), "len": (f, (bonds, bx, by, bz))}
    plan["d"] = (f, (bonds, bx, 3, by, bz))
    plan["hj"] = plan["hext"] = plan["hlen"] = (f, (halo, by, bz))
    plan["hd"] = (f, (halo, 3, by, bz))
    plan["mask"] = (f, (len(PAIRS), by, bz))
    plan["lanes"] = (f, (7, by, bz))
    plan["scaled"] = (f, (bonds, by, bz))
    plan["ix"] = (i, (bonds, H, rows, bz))
    plan["iy"] = (i, (bonds, bx, by, bz))
    plan["own_slots"] = (f, (len(SLOTS), by, bz))
    plan["slots"] = (f, (2, 2, len(TILES), rows, bz))
    plan["sent_slots"] = (f, (2, len(TILES), by, bz))
    for name, c in (("u", 3), ("t", 1)):
        plan[name, "field"] = (f, (c, planes, rows, bz))
        plan[name, "main"] = (f, (7, c, bx, rows, bz))
        plan[name, "sums"] = (f, (7, bx, c, rows, bz))
        plan[name, "base"] = (f, (c, bx, by, bz))
        plan[name, "x"] = (f, (7, c, 2 * H, rows, bz))
        plan[name, "y"] = (f, (7, c, 2 * H, planes, bz))
        plan[name, "in"] = (f, (c, by, bz))
        plan[name, "z"] = (f, (2, 3, c, rows, bz))
        plan[name, "q"] = (f, (len(MOVES), c, rows, bz))
    return plan


def kernel(sizes, names, u_hbm, intact_hbm, force_out, theta_out, *scratch):
    B = dict(zip(names, scratch))
    intact, send_sem, recv_sem, load_sem = scratch[len(names) :]
    bx, by, bz = theta_out.shape
    rows, planes = by + 2 * PAD, 2 * bx
    assert bx == by and planes * GROUP == bz and GROUP >= 2 * H + 2
    x_list, y_list, z_list = evaluations(bx, by)
    everything = x_list + y_list + z_list
    place = {e: i for i, e in enumerate(everything)}
    index = {a: lax.axis_index(a) for a in AXES}
    has = {(a, -1): index[a] > 0 for a in AXES}
    has.update({(a, 1): index[a] < sizes[a] - 1 for a in AXES})
    own = slice(PAD, PAD + by)

    def there(direction):
        found = None
        for a, step in zip(AXES, direction):
            if step:
                found = has[a, step] if found is None else found & has[a, step]
        return found

    everyone = [(x, y, z) for x in (-1, 0, 1) for y in (-1, 0, 1) for z in (-1, 0, 1) if x or y or z]
    exists = {d: there(d) for d in everyone}

    def device(direction):
        return {a: index[a] + step for a, step in zip(AXES, direction) if step}

    u = B["u", "field"]
    load_u = pltpu.make_async_copy(u_hbm, u.at[:, H : H + bx, own, :], load_sem.at[0])
    load_u.start()
    load = pltpu.make_async_copy(intact_hbm, intact, load_sem.at[1])
    load.start()

    barrier = pltpu.get_barrier_semaphore()
    count = jnp.int32(0)
    for d in sorted(everyone, key=lambda d: -sum(map(abs, d))):
        count = count + jnp.where(exists[d], 1, 0).astype(jnp.int32)

        @pl.when(exists[d])
        def _(d=d):
            pl.semaphore_signal(barrier, inc=1, device_id=device(d), device_id_type=MESH)

    copies = []

    class Shift:
        def __init__(self, direction, src, dst):
            number = len(copies)
            copies.append(self)
            self.direction = direction
            self.copy = pltpu.make_async_remote_copy(
                src_ref=src, dst_ref=dst, send_sem=send_sem.at[number], recv_sem=recv_sem.at[number],
                device_id=device(direction), device_id_type=MESH,
            )
            self.sends = exists[direction]
            self.takes = exists[minus(direction)]

            @pl.when(self.sends)
            def _():
                self.copy.start()

        def receive(self):
            @pl.when(self.takes)
            def _():
                self.copy.wait_recv()

        def finish(self):
            @pl.when(self.sends)
            def _():
                self.copy.wait_send()

    def nothing(view):
        view[...] = jnp.zeros(view.shape, view.dtype)

    def landing(name, d):
        if d[2]:
            return B[name, "z"].at[(d[2] + 1) // 2, d[0] + 1, :, side(d[1], by, PAD), :]
        return B[name, "field"].at[:, side(d[0], bx, H), side(d[1], by, PAD), :]

    SENT = (slice(0, by), slice(by - 2, by), slice(0, 2))
    LAND = (slice(PAD, PAD + by), slice(PAD - 2, PAD), slice(PAD + by, PAD + by + 2))
    up, down = span(lambda s: s[1] > 0), span(lambda s: s[1] < 0)
    x_all, x_up = span(lambda s: s[0] > 0), span(lambda s: s[0] > 0 and s[1] > 0)
    slot_moves = []
    for dz in (-1, 1):
        for dx, parts in ((0, (slice(0, len(TILES)), up, down)), (1, (x_all, x_up, down))):
            for way, dy in enumerate((0, 1, -1)):
                slot_moves.append(((dx, dy, dz), parts[way], way))

    def slot_landing(d, part, way):
        return B["slots"].at[(1 - d[2]) // 2, d[0], part, LAND[way], :]

    lane = lax.broadcasted_iota(jnp.int32, (by, bz), 1)
    row = lax.broadcasted_iota(jnp.int32, (by, bz), 0)
    spot = lax.rem(lane, GROUP)
    high = spot >= GROUP // 2
    edge = (lane < H) | (lane >= bz - H)
    inner = (lane >= H * GROUP) & (lane < (H + bx) * GROUP)
    zero = jnp.zeros((by, bz), jnp.float32)

    def number(condition):
        return jnp.where(condition, 1.0, 0.0)

    def roll(value, amount):
        return pltpu.roll(value, amount % bz, 1) if amount % bz else value

    def to_strip(total):
        return jnp.where(high, roll(total, GROUP), total)

    def pack(tiles):
        total = zero
        for x, tile in enumerate(tiles):
            total = total + roll(jnp.where(edge, tile, 0.0), GROUP * (x + H))
        return to_strip(total)

    def unpack(strip):
        strip = jnp.where(high, roll(strip, -GROUP), strip)
        return [jnp.where(edge, roll(strip, -GROUP * (x + H)), 0.0) for x in range(bx)]

    def flat(ref, *at):
        return ref.reshape(*ref.shape[:-3], ref.shape[-3] * ref.shape[-2], bz)

    u_flat, t_flat, intact_flat = flat(u), flat(B["t", "field"]), flat(intact)
    iy_flat = flat(B["iy"])

    def clear(ref, depth):
        zeros = jnp.zeros(ref.shape[2:], jnp.float32)

        def body(i, carry):
            for s in range(1, depth):
                ref[s, i] = zeros
            return carry

        lax.fori_loop(0, ref.shape[1], body, 0)

    def mask(ey, ez):
        return B["mask"][PAIRS.index((ey, ez))]

    def shift_main(name):
        field, out = B[name, "field"], B[name, "main"]

        def body(x, carry):
            for c in range(field.shape[0]):
                value = field[c, x + H, own, :]
                for ez in range(1 - H, H + 1):
                    moved = roll(value, -ez)
                    out[ez + H, c, x, own, :] = moved
                    out[ez + H, c, x, 0:PAD, :] = moved[0:PAD]
                    out[ez + H, c, x, PAD + by :, :] = moved[0:PAD]
            return carry

        lax.fori_loop(0, bx, body, 0)

    load_u.wait()
    for c in range(3):
        B["u", "in"][c] = pack([u[c, x + H, own, :] for x in range(bx)])
    load.wait()

    beyond_x = number(has["gx", 1])
    z_up, z_down = number(has["gz", 1]), number(has["gz", -1])

    def slots_body(x, totals):
        new = []
        crossing = jnp.where(has["gx", 1], 1.0, 0.0)
        for (ex, ey, az), total in zip(SLOTS, totals):
            value = jnp.where(lane >= bz - az, intact[NUMBER[ex, ey, az], x].astype(jnp.float32) * z_up, 0.0)
            if (ex, ey, -az) in NUMBER:
                other = intact[NUMBER[ex, ey, -az], x].astype(jnp.float32) * z_down
                value = jnp.where(lane < az, other, value)
            if ex:
                value = value * jnp.where(x + ex < bx, 1.0, crossing)
            new.append(total + pltpu.roll(value, GROUP * (x + H), 1))
        return tuple(new)

    totals = lax.fori_loop(0, bx, slots_body, tuple(zero for _ in SLOTS))
    y_inside = {}
    for ey in range(-H, H + 1):
        inside = (row + ey >= 0) & (row + ey < by)
        y_inside[ey] = jnp.where(inside, 1.0, number(has["gy", 1 if ey > 0 else -1])) if ey else None
    for (ex, ey, az), total in zip(SLOTS, totals):
        value = to_strip(total) * terms(NUMBER[ex, ey, az])[0]
        B["own_slots"][SLOT[ex, ey, az]] = value * y_inside[ey] if ey else value
    for i, (_, pair) in enumerate(TILES):
        one = B["own_slots"][SLOT[pair[0]]]
        for way, move in ((0, GROUP // 2), (1, -GROUP // 2)):
            value = one
            if len(pair) == 2:
                two = roll(B["own_slots"][SLOT[pair[1]]], move)
                value = jnp.where(high, one, two) if way else jnp.where(high, two, one)
            B["sent_slots"][way, i] = value

    pl.semaphore_wait(barrier, count)

    def spread(name):
        field, strip = B[name, "field"], B[name, "in"]
        sent = []
        for d in sorted(everyone, key=lambda d: -sum(map(abs, d))):
            if d[2]:
                src = strip.at[:, edge_of(d[1], by, 0), :]
            else:
                src = field.at[:, edge_of(d[0], bx, H), edge_of(d[1], by, PAD), :]
            sent.append(Shift(d, src, landing(name, minus(d))))
        return sent

    sent_u = spread("u")
    sent_i = []
    ends = {g: (slice(by - g[1], by) if g[1] > 0 else slice(0, -g[1])) for g in RUNS}
    for e, part, way in reversed(slot_moves):
        sent_i.append(Shift(e, B["sent_slots"].at[(e[2] + 1) // 2, part, SENT[way], :], slot_landing(e, part, way)))
    for (ex, ey), (k0, k1) in RUNS.items():
        src = intact.at[k0:k1, 0 : bx - ex, ends[ex, ey], :]
        sent_i.append(Shift((0, 1 if ey > 0 else -1, 0), src, B["iy"].at[k0:k1, ex:, ends[ex, ey], :]))
    for (ex, ey), (k0, k1) in RUNS.items():
        if ex:
            src = intact.at[k0:k1, bx - ex :, ends[ex, ey], :]
            sent_i.append(Shift((1, 1 if ey > 0 else -1, 0), src, B["iy"].at[k0:k1, 0:ex, ends[ex, ey], :]))
    for ex in range(1, H + 1):
        k0, k1 = FIRST[ex], LAST[ex]
        sent_i.append(Shift((1, 0, 0), intact.at[k0:k1, bx - ex :, :, :], B["ix"].at[k0:k1, 0:ex, own, :]))


    for d in everyone:

        @pl.when(jnp.logical_not(exists[d]))
        def _(d=d):
            for name in ("u", "t"):
                nothing(landing(name, d))
            for e, part, way in slot_moves:
                if minus(e) == d:
                    nothing(slot_landing(e, part, way))
            if d == (-1, 0, 0):
                for ex in range(1, H + 1):
                    nothing(B["ix"].at[FIRST[ex] : LAST[ex], 0:ex, own, :])
            for (ex, ey), (k0, k1) in RUNS.items():
                back = -1 if ey > 0 else 1
                at = slice(by - ey, by) if ey > 0 else slice(0, -ey)
                if d == (0, back, 0):
                    nothing(B["iy"].at[k0:k1, ex:, at, :])
                if ex and d == (-1, back, 0):
                    nothing(B["iy"].at[k0:k1, 0:ex, at, :])


    for i, (ey, ez) in enumerate(PAIRS):
        B["mask"][i] = number((row + ey >= 0) & (row + ey < by) & (lane + ez >= 0) & (lane + ez < bz))
    for ez in range(-H, H + 1):
        B["lanes"][ez + H] = number((lane + ez >= 0) & (lane + ez < bz))

    def blank_rows(i, carry):
        for name in ("u", "t"):
            out = B[name, "x"]
            for c in range(out.shape[1]):
                for s in range(7):
                    for part in (slice(0, PAD), slice(PAD + by, rows)):
                        out[s, c, i, part, :] = jnp.zeros((PAD, bz), jnp.float32)
        return carry

    lax.fori_loop(0, 2 * H, blank_rows, 0)

    clear(B["t", "sums"], 7)
    clear(B["u", "sums"], 7)
    for k, (ex, ey, ez) in enumerate(OFFSETS):
        B["scaled"][k] = mask(ey, ez) * terms(k)[0]

    shift_main("u")

    y_planes = {}
    for ex in range(H + 1):
        y_planes[ex] = jnp.where(row + ex < bx, 1.0, beyond_x)

    def own_flags(e):
        kind, at, step = e
        k, mine = bond_of(step)
        if kind == "x":
            return intact[k, at].astype(jnp.float32) * B["scaled"][k] * beyond_x
        value = intact_flat[k, pl.ds(at, bx, stride=by), :].astype(jnp.float32) * B["lanes"][step[2] + H]
        return value * (y_planes[step[0]] * (terms(k)[0] * number(has["gy", 1 if step[1] > 0 else -1])))

    for e in x_list + y_list:
        if bond_of(e[2])[1]:
            B["hj"][place[e]] = own_flags(e)

    def length(d, k):
        long2 = d[0] * d[0] + d[1] * d[1] + d[2] * d[2]
        return long2, long2 * lax.rsqrt(long2) - radius_of(k)

    acc_t, acc_f = B["t", "sums"], B["u", "sums"]
    uz, tz = B["u", "main"], B["t", "main"]

    groups = [[k for k in ORDER if OFFSETS[k][0] == ex] for ex in range(H + 1)]

    def dilate(part, x, carry):
        mine = [u[c, x + H, own, :] for c in range(3)]
        near = [{v: mine[c] - float(v) if v else mine[c] for v in range(-H, H + 1)} for c in range(3)]
        total = zero
        for k in part:
            ex, ey, ez = OFFSETS[k]
            at = slice(PAD + ey, PAD + ey + by)
            d = [uz[ez + H, c, x + ex, at, :] - near[c][OFFSETS[k][c]] for c in range(3)]
            long2, ext = length(d, k)
            flags = intact[k, x].astype(jnp.float32) * B["scaled"][k]
            term = flags * ext
            B["jf"][k, x] = flags
            for c in range(3):
                B["d"][k, x, c] = d[c]
            B["ext"][k, x] = ext
            B["len"][k, x] = long2
            total = total + term
            acc_t[ez + H, x + ex, 0, at, :] += term
        B["t", "base"][0, x] = total if OFFSETS[part[0]][0] == 0 else B["t", "base"][0, x] + total
        return carry

    for ex, part in enumerate(groups):
        lax.fori_loop(0, bx - ex, functools.partial(dilate, part), 0)

    def gather(name):
        sums, base = B[name, "sums"], B[name, "base"]

        def body(x, carry):
            for c in range(base.shape[0]):
                value = base[c, x] + sums[H, x, c, own, :]
                for ez in (-2, -1, 1, 2, 3):
                    value = value + roll(sums[ez + H, x, c, own, :], ez) * B["lanes"][H - ez]
                base[c, x] = value
            return carry

        lax.fori_loop(0, bx, body, 0)

    gather("t")

    def soften_one(j, ext, long2, k):
        _, p, q = terms(k)
        more = (ext * ext) * (1.0 / (radius_of(k) * soft_stretch) ** 2 / p) + 1.0 / p
        return j * lax.rsqrt(more * more * long2), ext * (q / p)

    NEEDED = (0, 2, 2, 2, 2, 0)

    def beside_x(name):
        field, out = B[name, "field"], B[name, "x"]
        for c in range(field.shape[0]):
            for i in range(2 * H):
                value = field[c, i if i < H else i + bx, own, :]
                for ez in range(-NEEDED[i], NEEDED[i] + 1):
                    out[ez + H, c, i, own, :] = roll(value, -ez)

    def beside_y(name):
        field_flat, out = flat(B[name, "field"]), B[name, "y"]
        for c in range(out.shape[1]):
            for i in range(2 * H):
                at = PAD - H + i if i < H else PAD + by + i - H
                for half in range(2):
                    value = field_flat[c, pl.ds(half * bx * rows + at, bx, stride=rows), :]
                    for ez in range(-NEEDED[i], NEEDED[i] + 1):
                        out[ez + H, c, i, half * bx : half * bx + bx, :] = roll(value, -ez)

    def beside_z(name):
        z, out = B[name, "z"], B[name, "q"]
        for c in range(out.shape[1]):
            for tile in (slice(0, by), slice(by, rows)):
                near, left, right = [jnp.where(high, z[0, i, c, tile, :], z[1, i, c, tile, :]) for i in (1, 0, 2)]
                far = roll(jnp.where(lane < bz // 2 - GROUP, right, left), bx * GROUP)
                value = jnp.where(inner, near, far)
                for i, (ex, az) in enumerate(MOVES):
                    over = roll(value, GROUP - GROUP * ex - az)
                    under = roll(value, -GROUP - GROUP * ex + az)
                    out[i, c, tile, :] = jnp.where(high, over, under)

    def receive(sent, kind):
        for copy in sent:
            dx, dy, dz = copy.direction
            if ("z" if dz else "y" if dy else "x") == kind:
                copy.receive()

    strip_sign = jnp.where(high, 1.0, -1.0)

    def other(name, e, c):
        kind, at, (ex, ey, ez) = e
        if kind == "x":
            i = at + ex + H if at + ex < 0 else at + ex - bx + H
            return B[name, "x"][ez + H, c, i, PAD + ey : PAD + ey + by, :]
        if kind == "y":
            i = at + ey + H if at + ey < 0 else at + ey - by + H
            return B[name, "y"][ez + H, c, i, H + ex : H + ex + bx, :]
        return B[name, "q"][MOVES.index((ex, ez)), c, PAD + ey : PAD + ey + by, :]

    def inside(name, kind, at, c):
        if kind == "x":
            return B[name, "field"][c, at + H, own, :]
        if kind == "y":
            flat_field = u_flat if name == "u" else t_flat
            return flat_field[c, pl.ds(H * rows + PAD + at, bx, stride=rows), :]
        return B[name, "in"][c]

    def bond(e):
        return NUMBER[e[2]] if e[0] == "z" and e[2] in NUMBER else bond_of(e[2])[0]

    def add(name, kind, at, totals):
        base = B[name, "base"]
        for c, total in enumerate(totals):
            if kind == "x":
                base[c, at] += total
            else:
                base_flat = flat(base)
                base_flat[c, pl.ds(at, bx, stride=by), :] += total

    def stretch(part, flags_known):
        near, was, total = {}, None, None
        for e in part:
            kind, at, step = e
            if (kind, at) != was:
                if was is not None and flags_known:
                    add("t", *was, [total])
                was, near, total = (kind, at), {}, None
            i, k = place[e], bond(e)
            d = []
            for c in range(3):
                if (c, step[c]) not in near:
                    if (c, None) not in near:
                        near[c, None] = inside("u", kind, at, c)
                    start = near[c, None]
                    if step[c]:
                        move = strip_sign * float(step[c]) if kind == "z" and c == 2 else float(step[c])
                        start = start - move
                    near[c, step[c]] = start
                d.append(other("u", e, c) - near[c, step[c]])
            long2, ext = length(d, k)
            for c in range(3):
                B["hd"][i, c] = d[c]
            B["hext"][i] = ext
            B["hlen"][i] = long2
            if flags_known:
                term = B["hj"][i] * ext
                total = total + term if total is not None else term
        if flags_known:
            add("t", *was, [total])

    def weigh(part, flags_of):
        was, total = None, None
        for e in part:
            if e[:2] != was:
                if was is not None:
                    add("t", *was, [total])
                was, total = e[:2], None
            flags = flags_of(e)
            B["hj"][place[e]] = flags
            term = flags * B["hext"][place[e]]
            total = total + term if total is not None else term
        if was[0] == "z":
            return total
        add("t", *was, [total])

    def from_slots(ex, ey, az):
        got, (s, second) = B["slots"], WHERE[ex, ey, az]
        part = slice(PAD - ey, PAD - ey + by)
        a, b, move = (1, 0, GROUP // 2) if second else (0, 1, 0)
        value = jnp.where(high, got[a, 0, s, part, :], got[b, 0, s, part, :])
        if ex:
            far = jnp.where(high, got[a, 1, s, part, :], got[b, 1, s, part, :])
            value = jnp.where(inner, value, roll(far, bx * GROUP))
        over = roll(value, GROUP + GROUP * ex - az - move)
        under = roll(value, -GROUP + GROUP * ex + az + move)
        return jnp.where(spot >= GROUP - az, over, jnp.where(spot < az, under, 0.0))

    def taken_flags(e):
        kind, at, step = e
        ex, ey, ez = minus(step)
        k = NUMBER[ex, ey, ez]
        if kind == "x":
            value = B["ix"][k, at, PAD - ey : PAD - ey + by, :].astype(jnp.float32)
            return roll(value, ez) * (mask(*step[1:]) * terms(k)[0])
        from_row = at - ey + by if ey > 0 else at - ey - by
        value = iy_flat[k, pl.ds(from_row, bx, stride=by), :].astype(jnp.float32)
        return roll(value, ez) * (B["lanes"][step[2] + H] * terms(k)[0])

    own_x, taken_x = [[e for e in x_list if bond_of(e[2])[1] == mine] for mine in (True, False)]
    own_y, taken_y = [[e for e in y_list if bond_of(e[2])[1] == mine] for mine in (True, False)]

    def strip_flags(e):
        ex, ey, az = e[2]
        value = B["own_slots"][SLOT[e[2]]] if e[2] in SLOT else None
        if (-ex, -ey, az) in SLOT:
            more = from_slots(-ex, -ey, az)
            value = more if value is None else value + more
        return value

    receive(sent_u, "x")
    beside_x("u")
    stretch(own_x, True)
    stretch(taken_x, False)
    receive(sent_u, "y")
    beside_y("u")
    stretch(own_y, True)
    stretch(taken_y, False)
    receive(sent_u, "z")
    beside_z("u")
    stretch(z_list, False)
    receive(sent_i, "x")
    weigh(taken_x, taken_flags)
    receive(sent_i, "z")
    strip_t = weigh(z_list, strip_flags)
    receive(sent_i, "y")
    weigh(taken_y, taken_flags)

    def finish(name, c, strip, write):
        base = B[name, "base"]
        for x, part in enumerate(unpack(strip)):
            write(x, base[c, x] + part)

    t = B["t", "field"]

    def write_theta(x, value):
        theta_out[x] = value
        t[0, x + H, own, :] = value

    B["t", "in"][0] = pack([B["t", "base"][0, x] for x in range(bx)]) + strip_t
    finish("t", 0, strip_t, write_theta)
    sent_t = spread("t")

    shift_main("t")

    def push(part, x, carry):
        here = t[0, x + H, own, :]
        total = [zero, zero, zero]
        for k in part:
            ex, ey, ez = OFFSETS[k]
            at = slice(PAD + ey, PAD + ey + by)
            g, h = soften_one(B["jf"][k, x], B["ext"][k, x], B["len"][k, x], k)
            scalar = g * (here + tz[ez + H, 0, x + ex, at, :] + h)
            for c in range(3):
                pushed = scalar * B["d"][k, x, c]
                total[c] = total[c] + pushed
                acc_f[ez + H, x + ex, c, at, :] -= pushed
        for c in range(3):
            B["u", "base"][c, x] = total[c] if OFFSETS[part[0]][0] == 0 else B["u", "base"][c, x] + total[c]
        return carry

    for ex, part in enumerate(groups):
        lax.fori_loop(0, bx - ex, functools.partial(push, part), 0)
    gather("u")
    for e in everything:
        i = place[e]
        B["hlen"][i], B["hext"][i] = soften_one(B["hj"][i], B["hext"][i], B["hlen"][i], bond(e))

    for copy in copies:
        copy.finish()

    def forces(part):
        was, total = None, None
        for e in part:
            kind, at, _ = e
            if (kind, at) != was:
                if was is not None:
                    add("u", *was, total)
                was, total = (kind, at), None
                here = inside("t", kind, at, 0)
            i = place[e]
            scalar = B["hlen"][i] * (here + other("t", e, 0) + B["hext"][i])
            pushed = [scalar * B["hd"][i, c] for c in range(3)]
            total = [total[c] + pushed[c] for c in range(3)] if total is not None else pushed
        if was[0] == "z":
            return total
        add("u", *was, total)

    receive(sent_t, "x")
    beside_x("t")
    forces(x_list)
    receive(sent_t, "y")
    beside_y("t")
    forces(y_list)
    receive(sent_t, "z")
    beside_z("t")
    strip_f = forces(z_list)

    for c in range(3):

        def write_force(x, value, c=c):
            force_out[c, x] = value

        finish("u", c, strip_f[c], write_force)


def shards(sizes, displacement, bond_intact):
    plan = scratch_plan(bond_intact.shape[0], *displacement.shape[1:])
    scratch = [pltpu.VMEM(shape, dtype) for dtype, shape in plan.values()]
    scratch += [
        pltpu.VMEM(bond_intact.shape, jnp.int32),
        pltpu.SemaphoreType.DMA((96,)),
        pltpu.SemaphoreType.DMA((96,)),
        pltpu.SemaphoreType.DMA((2,)),
    ]
    vmem, anywhere = pl.BlockSpec(memory_space=pltpu.VMEM), pl.BlockSpec(memory_space=pl.ANY)
    return pl.pallas_call(
        functools.partial(kernel, sizes, tuple(plan)),
        out_shape=(
            jax.ShapeDtypeStruct(displacement.shape, jnp.float32),
            jax.ShapeDtypeStruct(displacement.shape[1:], jnp.float32),
        ),
        in_specs=[anywhere, anywhere],
        out_specs=(vmem, vmem),
        scratch_shapes=scratch,
        compiler_params=pltpu.CompilerParams(collective_id=0, has_side_effects=True, vmem_limit_bytes=56375000),
    )(displacement, bond_intact)


def solution(mesh):
    sizes = {a: mesh.shape[a] for a in AXES}
    return jax.shard_map(
        functools.partial(shards, sizes),
        mesh=mesh,
        in_specs=(P(None, "gx", "gy", "gz"), P(None, "gx", "gy", "gz")),
        out_specs=(P(None, "gx", "gy", "gz"), P("gx", "gy", "gz")),
        check_vma=False,
    )
```
